512 devices in a mesh: hist: 32 (over x, y, core), second: 16 (over z).
Axes of the slice: x: 4, y: 4, z: 16, core: 2. Of those that a mesh axis runs over, the one named last changes fastest.
Arguments:
- history: bfloat16 [32768, 32768], P('hist', 'second'), may hold values from -0.03125 to 0.03125
- self_rows: bfloat16 [256, 32768], P(None, 'hist'), may hold values from -6 to 6
- edge_rows: bfloat16 [128, 32768], P(None, 'second'), may hold values from -6 to 6
- step_inv: float32 [128, 128], replicated, may hold values from -0.08 to 0.98, as said below
- coupling: float32 [128], replicated, may hold values from 0.1 to 1
- reach: int32 [3, 256], replicated, may hold values from 1 to 256, as said below
Outputs:
- green_last: bfloat16 [256, 32768], P(None, 'second')
The draws below stay inside these ranges and needn't reach their ends.
Inputs may be any that keep to these rules, and one draw needn't show every extreme that they name: `step_inv`: entries other than the diagonal lie within 0.08 of zero; diagonal entries between 0.5 and 0.9. reach[b, c] is at least c + 1 and at most min(256, c + 2 * b + 4).
All inputs are finite; a program needn't handle non-finite values.
Results may differ from the reference program's by a relative error of at most 0.014.
Values may be sent and summed in bfloat16 or wider, within the bound.
No kernel may reach another device: no remote copies, remote signals or barrier semaphores. Data moves between devices by JAX's collectives and lax.ppermute only.
A program may use at most 64 MiB of HBM per device.

```python
import math
import jax
import jax.numpy as jnp
from jax import lax

TPB = 2
NBLK = 3
ROW_T = 128
ROWS = 256
P_SIZE = 256
KH = 32768
N_HIST = 32


def draw_step_inv(key, part):
    first_key, second_key = jax.random.split(jax.random.fold_in(key, 11))
    diagonal = jax.random.uniform(first_key, (ROW_T,), jnp.float32, 0.5, 0.9)
    spread = 0.25 / ROW_T ** 0.5
    others = jax.random.normal(second_key, (ROW_T, ROW_T), jnp.float32) * spread
    others = jnp.clip(others, -0.08, 0.08)
    others = others * (1.0 - jnp.eye(ROW_T, dtype=jnp.float32))
    return (others + jnp.diag(diagonal)).astype(jnp.float32)


def draw_reach(key, part):
    offsets = jax.random.randint(jax.random.fold_in(key, 23), (NBLK, P_SIZE), 0, 4)
    columns = jnp.arange(P_SIZE, dtype=jnp.int32)[None, :]
    sections = jnp.arange(NBLK, dtype=jnp.int32)[:, None]
    return jnp.minimum(columns + 1 + 2 * sections + offsets, P_SIZE).astype(jnp.int32)


def block_levels(rng, dims, cuts, smallest, largest):
    factor_of, own = 1.0, jax.random.fold_in(rng, 6)
    for position, shards_of in cuts:
        steps = jnp.exp(jax.random.uniform(jax.random.fold_in(own, position), (shards_of,), jnp.float32, smallest / len(cuts), largest / len(cuts)))
        factor_of = factor_of * jnp.repeat(steps, dims[position] // shards_of).reshape([-1 if axis == position else 1 for axis in range(len(dims))])
    return factor_of


def bell_draw(stream_key, dims, scale, most, cuts=(), held_as=jnp.bfloat16):
    result = scale * jax.random.normal(stream_key, dims, jnp.float32)
    if cuts:
        result = result * block_levels(stream_key, dims, cuts, -0.22, 0.18)
    return jnp.clip(result, -most, most).astype(held_as)


def setup_inputs(seed: int = 0) -> dict:
    seeds = jax.random.split(jax.random.key(seed), 7)
    history = bell_draw(seeds[0], (KH, KH), KH ** -0.5, 0.03125, ((0, 32), (1, 16)))
    self_rows = bell_draw(seeds[1], (ROWS, KH), 1.0, 6.0, ((1, 32),))
    edge_rows = bell_draw(seeds[2], (ROW_T, KH), 1.0, 6.0, ((1, 16),))
    step_inv = draw_step_inv(jax.random.fold_in(seeds[6], 71), 0)
    coupling = jnp.clip(jnp.exp(jax.random.uniform(seeds[4], (ROW_T,), jnp.float32, math.log(0.1), math.log(1.0))), 0.1, 1.0)
    reach = draw_reach(jax.random.fold_in(seeds[6], 71), 0)
    return {"history": history, "self_rows": self_rows, "edge_rows": edge_rows, "step_inv": step_inv, "coupling": coupling, "reach": reach}


def screened(block_rows, weights):
    square = block_rows * block_rows
    return weights[:, None] * block_rows * square / (1.0 + square)


def reference(history, self_rows, edge_rows, step_inv, coupling, reach):
    slab_rows = KH // N_HIST
    past_slab = slab_rows // ROW_T
    shards = history.reshape(N_HIST, slab_rows, KH)
    starts = jnp.arange(N_HIST, dtype=jnp.int32) * past_slab
    weights = jnp.tile(coupling, TPB)
    sigma_rows = self_rows
    green_now = edge_rows.astype(jnp.float32)
    finished = None
    for moment in range(NBLK):
        limit_row = reach[moment]
        pieces = jnp.moveaxis(sigma_rows.reshape(ROWS, N_HIST, slab_rows), 1, 0)

        def add_shard(running, inputs):
            rows_hist, left_rows, first_past = inputs
            past_ids = first_past + jnp.arange(past_slab, dtype=jnp.int32)
            live_mask = past_ids[:, None] < limit_row[None, :]
            masked = jnp.where(live_mask[:, None, :, None], rows_hist.reshape(past_slab, ROW_T, P_SIZE, ROW_T),
                               jnp.zeros((), rows_hist.dtype)).reshape(slab_rows, KH)
            shard_term = jnp.dot(left_rows.astype(jnp.float32), masked.astype(jnp.float32),
                                 precision=lax.Precision.HIGHEST, preferred_element_type=jnp.float32)
            rounded = lax.optimization_barrier(shard_term.astype(jnp.bfloat16))
            return running + rounded.astype(jnp.float32), None

        integral, _ = lax.scan(add_shard, jnp.zeros((ROWS, KH), jnp.float32), (shards, pieces, starts))
        rows_out = []
        for step_number in range(TPB):
            source = green_now + integral[step_number * ROW_T:(step_number + 1) * ROW_T]
            green_now = jnp.dot(step_inv, source, precision=lax.Precision.HIGHEST,
                                preferred_element_type=jnp.float32)
            rows_out.append(green_now)
        block_rows = jnp.concatenate(rows_out, 0)
        if moment + 1 < NBLK:
            sigma_rows = screened(block_rows, weights).astype(jnp.bfloat16)
        else:
            finished = block_rows.astype(jnp.bfloat16)
    return finished
```

```python
import functools

import jax
import jax.numpy as jnp
from jax import lax
from jax.experimental import pallas as pl
from jax.experimental.pallas import tpu as pltpu
from jax.sharding import Mesh
from jax.sharding import PartitionSpec as P

HIST = ("x", "y", "c")
PLANE = ("x", "y")
ROW_T = 128
HALF = 64
TILE = 256


def low_lanes(shape):
    return lax.broadcasted_iota(jnp.int32, shape, 1) < HALF


def swap_halves(value):
    return pltpu.roll(value, HALF, 1)


def unpack_pair(even, odd):
    low = low_lanes(even.shape)
    return (
        jnp.where(low, even, swap_halves(odd)),
        jnp.where(low, swap_halves(even), odd),
    )


def memory_kernel(block, first_half, from_pieces, where_ref, reach_ref, sigma_ref, hist_ref, out_ref, *scratch):
    rows, cols = hist_ref.shape
    past_loc, tiles = rows // ROW_T, cols // ROW_T
    hist_place, second_place, own = where_ref[0], where_ref[1], where_ref[2]
    half = 1 - own if first_half else own
    step = pl.program_id(0)
    if from_pieces:
        sigma = scratch[0]

        @pl.when(step == 0)
        def _():
            for pair in range(sigma_ref.shape[0] // 2):
                top, bottom = unpack_pair(
                    sigma_ref[2 * pair].astype(jnp.float32), sigma_ref[2 * pair + 1].astype(jnp.float32)
                )
                sigma[:ROW_T, pair * ROW_T : (pair + 1) * ROW_T] = top.astype(jnp.bfloat16)
                sigma[ROW_T:, pair * ROW_T : (pair + 1) * ROW_T] = bottom.astype(jnp.bfloat16)
    else:
        sigma = sigma_ref
    tile_0 = second_place * 16 + half * 8 + step * tiles
    columns = []
    for tile in range(tiles):
        live = reach_ref[block, tile_0 + tile] - hist_place * past_loc
        columns.append(
            jnp.concatenate(
                [
                    jnp.where(
                        past < live,
                        hist_ref[past * ROW_T : (past + 1) * ROW_T, tile * ROW_T : (tile + 1) * ROW_T],
                        jnp.zeros((), hist_ref.dtype),
                    )
                    for past in range(past_loc)
                ],
                0,
            )
        )
    masked = jnp.concatenate(columns, 1)
    term = jnp.dot(sigma[...], masked, preferred_element_type=jnp.float32)
    for tile in range(tiles):
        top = term[:ROW_T, tile * ROW_T : (tile + 1) * ROW_T]
        bottom = term[ROW_T:, tile * ROW_T : (tile + 1) * ROW_T]
        even, odd = unpack_pair(top, bottom)
        out_ref[2 * tile] = even.astype(out_ref.dtype)
        out_ref[2 * tile + 1] = odd.astype(out_ref.dtype)


def memory_terms(block, first_half, where, reach, sigma, history):
    rows, cols = history.shape
    from_pieces = sigma.ndim == 3
    steps = cols // 2 // TILE

    def hist_map(i, where_ref, reach_ref):
        own = where_ref[2]
        return (0, ((1 - own) if first_half else own) * steps + i)

    return pl.pallas_call(
        functools.partial(memory_kernel, block, first_half, from_pieces),
        out_shape=jax.ShapeDtypeStruct((cols // 2 // HALF, ROW_T, ROW_T), jnp.bfloat16),
        grid_spec=pltpu.PrefetchScalarGridSpec(
            num_scalar_prefetch=2,
            grid=(steps,),
            in_specs=[
                pl.BlockSpec(sigma.shape, lambda i, w, r: (0,) * sigma.ndim),
                pl.BlockSpec((rows, TILE), hist_map),
            ],
            out_specs=pl.BlockSpec((TILE // HALF, ROW_T, ROW_T), lambda i, w, r: (i, 0, 0)),
            scratch_shapes=[pltpu.VMEM((2 * ROW_T, rows), jnp.bfloat16)] if from_pieces else [],
        ),
        cost_estimate=pl.CostEstimate(
            flops=2 * 256 * rows * cols // 2, bytes_accessed=rows * cols + 1024 * 1024, transcendentals=0
        ),
        name=f"memory_{block}_{int(first_half)}",
    )(where, reach, sigma, history)


def step_kernel(first, last, where_ref, terms_ref, green_ref, step_ref, weight_ref, *outs):
    integral = terms_ref[0].astype(jnp.float32)
    for piece in range(1, terms_ref.shape[0]):
        integral = integral + terms_ref[piece].astype(jnp.float32)
    low = low_lanes(integral.shape)
    held = green_ref[...].astype(jnp.float32)
    turned = swap_halves(held)
    if first:
        before = jnp.where(where_ref[3] == 0, held, turned)
    else:
        before = turned
    source = integral + jnp.where(low, before, 0.0)
    dot = functools.partial(jnp.dot, precision=lax.Precision.HIGHEST, preferred_element_type=jnp.float32)
    moved = dot(step_ref[...], source)
    further = dot(step_ref[...], jnp.where(low, 0.0, swap_halves(moved)))
    rows = moved + further
    if last:
        piece = rows.astype(jnp.bfloat16)
    else:
        square = rows * rows
        piece = (weight_ref[...] * rows * square / (1.0 + square)).astype(jnp.bfloat16)
        outs[1][...] = rows
    for copy in range(outs[0].shape[0]):
        outs[0][copy] = piece


def advance(first, last, where, terms, green, step_inv, weights):
    whole = pl.BlockSpec(memory_space=pltpu.VMEM)
    shapes = [jax.ShapeDtypeStruct((16, ROW_T, ROW_T), jnp.bfloat16)]
    specs = [pl.BlockSpec((16, ROW_T, ROW_T), lambda i, w: (0, 0, 0))]
    if not last:
        shapes.append(jax.ShapeDtypeStruct((ROW_T, ROW_T), jnp.float32))
        specs.append(pl.BlockSpec((ROW_T, ROW_T), lambda i, w: (0, 0)))
    square = pl.BlockSpec((ROW_T, ROW_T), lambda i, w: (0, 0))
    green_spec = pl.BlockSpec((ROW_T, ROW_T), lambda i, w: (0, w[4])) if first else square
    out = pl.pallas_call(
        functools.partial(step_kernel, first, last),
        out_shape=tuple(shapes),
        grid_spec=pltpu.PrefetchScalarGridSpec(
            num_scalar_prefetch=1,
            grid=(1,),
            in_specs=[pl.BlockSpec(terms.shape, lambda i, w: (0, 0, 0)), green_spec, square, square],
            out_specs=tuple(specs),
        ),
        name=f"advance_{int(first)}{int(last)}",
    )(where, terms, green, step_inv, weights)
    return out[0], (None if last else out[1])


def spread_kernel(where_ref, own_ref, other_ref, out_ref):
    step = pl.program_id(0)
    mine = where_ref[2] == (step >= 8).astype(jnp.int32)

    def write(ref):
        top, bottom = unpack_pair(ref[0].astype(jnp.float32), ref[1].astype(jnp.float32))
        out_ref[:ROW_T] = top.astype(out_ref.dtype)
        out_ref[ROW_T:] = bottom.astype(out_ref.dtype)

    @pl.when(mine)
    def _():
        write(own_ref)

    @pl.when(jnp.logical_not(mine))
    def _():
        write(other_ref)


def spread_out(where, own, other):
    pair = pl.BlockSpec((2, ROW_T, ROW_T), lambda i, w: (lax.rem(i, 8), 0, 0))
    return pl.pallas_call(
        spread_kernel,
        out_shape=jax.ShapeDtypeStruct((2 * ROW_T, 16 * ROW_T), jnp.bfloat16),
        grid_spec=pltpu.PrefetchScalarGridSpec(
            num_scalar_prefetch=1,
            grid=(16,),
            in_specs=[pair, pair],
            out_specs=pl.BlockSpec((2 * ROW_T, ROW_T), lambda i, w: (0, i)),
        ),
        name="spread",
    )(where, own, other)


def exchange(x, axis):
    return lax.all_to_all(x, axis, 0, 0, tiled=True)


def local(history, self_rows, edge_rows, step_inv, coupling, reach):
    place = lax.axis_index(PLANE)
    core = lax.axis_index("c")
    where = jnp.stack(
        [lax.axis_index(HIST), lax.axis_index("z"), core, place % 2, core * 8 + place // 2]
    ).astype(jnp.int32)
    weights = jnp.broadcast_to(coupling[:, None], (ROW_T, ROW_T))
    swap = [(0, 1), (1, 0)]
    sigma, green = self_rows, edge_rows
    blocks = reach.shape[0]
    for block in range(blocks):
        last = block + 1 == blocks
        away = memory_terms(block, True, where, reach, sigma, history)
        arrived = lax.ppermute(away, "c", swap)
        kept = memory_terms(block, False, where, reach, sigma, history)
        pair = (kept.astype(jnp.float32) + arrived.astype(jnp.float32)).astype(jnp.bfloat16)
        terms = exchange(pair, PLANE)
        pieces, green = advance(block == 0, last, where, terms, green, step_inv, weights)
        if last:
            own = exchange(pieces, PLANE)
            return spread_out(where, own, lax.ppermute(own, "c", swap))
        sigma = exchange(exchange(pieces, "z"), PLANE)


def solution(mesh):
    torus = Mesh(mesh.devices.reshape(4, 4, 2, mesh.shape["second"]), ("x", "y", "c", "z"))
    placed = (P(HIST, "z"), P(None, HIST), P(None, "z"), P(), P(), P())
    return jax.shard_map(local, mesh=torus, in_specs=placed, out_specs=P(None, "z"), check_vma=False)
```

```python
import functools

import jax
import jax.numpy as jnp
from jax import lax
from jax.experimental import pallas as pl
from jax.experimental.pallas import tpu as pltpu
from jax.sharding import Mesh
from jax.sharding import PartitionSpec as P

HIST = ("x", "y", "c")
PLANE = ("x", "y")
ROW_T = 128
HALF = 64
TILE = 256


def low_lanes(shape):
    return lax.broadcasted_iota(jnp.int32, shape, 1) < HALF


def swap_halves(value):
    return pltpu.roll(value, HALF, 1)


def unpack_pair(even, odd):
    low = low_lanes(even.shape)
    return (
        jnp.where(low, even, swap_halves(odd)),
        jnp.where(low, swap_halves(even), odd),
    )


VMEM = pl.BlockSpec(memory_space=pltpu.VMEM)
SMEM = pl.BlockSpec(memory_space=pltpu.SMEM)
PARAMS = pltpu.CompilerParams(vmem_limit_bytes=16 * 1024 * 1024)


def memory_kernel(block, first_half, from_pieces, reach_ref, sigma_ref, hist_ref, out_ref, *scratch):
    rows = hist_ref.shape[0]
    past_loc, tiles = rows // ROW_T, TILE // ROW_T
    hist_place, second_place, own = lax.axis_index(HIST), lax.axis_index("z"), lax.axis_index("c")
    half = 1 - own if first_half else own
    if from_pieces:
        sigma = scratch[0]
        for pair in range(sigma_ref.shape[0] // 2):
            top, bottom = unpack_pair(
                sigma_ref[2 * pair].astype(jnp.float32), sigma_ref[2 * pair + 1].astype(jnp.float32)
            )
            sigma[:ROW_T, pair * ROW_T : (pair + 1) * ROW_T] = top.astype(jnp.bfloat16)
            sigma[ROW_T:, pair * ROW_T : (pair + 1) * ROW_T] = bottom.astype(jnp.bfloat16)
    else:
        sigma = sigma_ref
    steps = hist_ref.shape[1] // 2 // TILE
    for step in range(steps):
        start = pl.multiple_of((half * steps + step) * TILE, TILE)
        tile_0 = second_place * 16 + half * 8 + step * tiles
        columns = []
        for tile in range(tiles):
            live = reach_ref[block, tile_0 + tile] - hist_place * past_loc
            columns.append(
                jnp.concatenate(
                    [
                        jnp.where(
                            past < live,
                            hist_ref[past * ROW_T : (past + 1) * ROW_T, pl.ds(start + tile * ROW_T, ROW_T)],
                            jnp.zeros((), hist_ref.dtype),
                        )
                        for past in range(past_loc)
                    ],
                    0,
                )
            )
        masked = jnp.concatenate(columns, 1)
        term = jnp.dot(sigma[...], masked, preferred_element_type=jnp.float32)
        for tile in range(tiles):
            top = term[:ROW_T, tile * ROW_T : (tile + 1) * ROW_T]
            bottom = term[ROW_T:, tile * ROW_T : (tile + 1) * ROW_T]
            even, odd = unpack_pair(top, bottom)
            out_ref[(step * tiles + tile) * 2] = even.astype(out_ref.dtype)
            out_ref[(step * tiles + tile) * 2 + 1] = odd.astype(out_ref.dtype)


def memory_terms(block, first_half, reach, sigma, history):
    rows, cols = history.shape
    from_pieces = sigma.ndim == 3
    return pl.pallas_call(
        functools.partial(memory_kernel, block, first_half, from_pieces),
        out_shape=jax.ShapeDtypeStruct((cols // 2 // HALF, ROW_T, ROW_T), jnp.bfloat16),
        in_specs=[SMEM, VMEM, VMEM],
        out_specs=VMEM,
        scratch_shapes=[pltpu.VMEM((2 * ROW_T, rows), jnp.bfloat16)] if from_pieces else [],
        cost_estimate=pl.CostEstimate(
            flops=2 * 256 * rows * cols // 2, bytes_accessed=rows * cols + 1024 * 1024, transcendentals=0
        ),
        compiler_params=PARAMS,
        name=f"memory_{block}_{int(first_half)}",
    )(reach, sigma, history)


def step_kernel(first, last, terms_ref, green_ref, step_ref, coupling_ref, *outs):
    integral = terms_ref[0].astype(jnp.float32)
    for piece in range(1, terms_ref.shape[0]):
        integral = integral + terms_ref[piece].astype(jnp.float32)
    low = low_lanes(integral.shape)
    if first:
        place = lax.axis_index("x") * 4 + lax.axis_index("y")
        tile = pl.multiple_of((lax.axis_index("c") * 8 + place // 2) * ROW_T, ROW_T)
        held = green_ref[:, pl.ds(tile, ROW_T)].astype(jnp.float32)
        before = jnp.where(place % 2 == 0, held, swap_halves(held))
    else:
        before = swap_halves(green_ref[...])
    source = integral + jnp.where(low, before, 0.0)
    dot = functools.partial(jnp.dot, precision=lax.Precision.HIGHEST, preferred_element_type=jnp.float32)
    moved = dot(step_ref[...], source)
    further = dot(step_ref[...], jnp.where(low, 0.0, swap_halves(moved)))
    rows = moved + further
    if last:
        piece = rows.astype(jnp.bfloat16)
    else:
        square = rows * rows
        piece = (coupling_ref[...] * rows * square / (1.0 + square)).astype(jnp.bfloat16)
        outs[1][...] = rows
    for copy in range(outs[0].shape[0]):
        outs[0][copy] = piece


def advance(first, last, terms, green, step_inv, coupling):
    shapes = [jax.ShapeDtypeStruct((16, ROW_T, ROW_T), jnp.bfloat16)]
    if not last:
        shapes.append(jax.ShapeDtypeStruct((ROW_T, ROW_T), jnp.float32))
    out = pl.pallas_call(
        functools.partial(step_kernel, first, last),
        out_shape=tuple(shapes),
        in_specs=[VMEM, VMEM, VMEM, VMEM],
        out_specs=(VMEM,) * len(shapes),
        compiler_params=PARAMS,
        name=f"advance_{int(first)}{int(last)}",
    )(terms, green, step_inv, coupling)
    return out[0], (None if last else out[1])


def spread_kernel(own_ref, other_ref, out_ref):
    def write(ref, half):
        for pair in range(8):
            top, bottom = unpack_pair(ref[2 * pair].astype(jnp.float32), ref[2 * pair + 1].astype(jnp.float32))
            start = pl.multiple_of((half * 8 + pair) * ROW_T, ROW_T)
            out_ref[:ROW_T, pl.ds(start, ROW_T)] = top.astype(out_ref.dtype)
            out_ref[ROW_T:, pl.ds(start, ROW_T)] = bottom.astype(out_ref.dtype)

    core = lax.axis_index("c")
    write(own_ref, core)
    write(other_ref, 1 - core)


def spread_out(own, other):
    return pl.pallas_call(
        spread_kernel,
        out_shape=jax.ShapeDtypeStruct((2 * ROW_T, 16 * ROW_T), jnp.bfloat16),
        in_specs=[VMEM, VMEM],
        out_specs=VMEM,
        compiler_params=PARAMS,
        name="spread",
    )(own, other)


def exchange(x, axis):
    return lax.all_to_all(x, axis, 0, 0, tiled=True)


def local(history, self_rows, edge_rows, step_inv, coupling, reach):
    weights = coupling[:, None]
    swap = [(0, 1), (1, 0)]
    sigma, green = self_rows, edge_rows
    blocks = reach.shape[0]
    for block in range(blocks):
        last = block + 1 == blocks
        away = memory_terms(block, True, reach, sigma, history)
        arrived = lax.ppermute(away, "c", swap)
        kept = memory_terms(block, False, reach, sigma, history)
        pair = (kept.astype(jnp.float32) + arrived.astype(jnp.float32)).astype(jnp.bfloat16)
        terms = exchange(pair, PLANE)
        pieces, green = advance(block == 0, last, terms, green, step_inv, weights)
        if last:
            own = exchange(pieces, PLANE)
            return spread_out(own, lax.ppermute(own, "c", swap))
        sigma = exchange(exchange(pieces, "z"), PLANE)


def solution(mesh):
    torus = Mesh(mesh.devices.reshape(4, 4, 2, mesh.shape["second"]), ("x", "y", "c", "z"))
    placed = (P(HIST, "z"), P(None, HIST), P(None, "z"), P(), P(), P())
    return jax.shard_map(local, mesh=torus, in_specs=placed, out_specs=P(None, "z"), check_vma=False)
```

```python
import functools

import jax
import jax.numpy as jnp
from jax import lax
from jax.experimental import pallas as pl
from jax.experimental.pallas import tpu as pltpu
from jax.sharding import Mesh
from jax.sharding import PartitionSpec as P

HIST = ("x", "y", "c")
PLANE = ("y", "x")
SECOND = ("far", "near")
ROW_T = 128
HALF = 64
TILE = 256


def low_lanes(shape):
    return lax.broadcasted_iota(jnp.int32, shape, 1) < HALF


def swap_halves(value):
    return pltpu.roll(value, HALF, 1)


def unpack_pair(even, odd):
    low = low_lanes(even.shape)
    return (
        jnp.where(low, even, swap_halves(odd)),
        jnp.where(low, swap_halves(even), odd),
    )


VMEM = pl.BlockSpec(memory_space=pltpu.VMEM)
SMEM = pl.BlockSpec(memory_space=pltpu.SMEM)
PARAMS = pltpu.CompilerParams(vmem_limit_bytes=16 * 1024 * 1024)


def column_tile(block, half, step, reach_ref, sigma, hist_ref, out_ref):
    past_loc, tiles = hist_ref.shape[0] // ROW_T, TILE // ROW_T
    steps = hist_ref.shape[1] // 2 // TILE
    start = pl.multiple_of((half * steps + step) * TILE, TILE)
    tile_0 = lax.axis_index(SECOND) * (2 * steps * tiles) + (half * steps + step) * tiles
    columns = []
    for tile in range(tiles):
        live = reach_ref[block, tile_0 + tile] - lax.axis_index(HIST) * past_loc
        columns.append(
            jnp.concatenate(
                [
                    jnp.where(
                        past < live,
                        hist_ref[past * ROW_T : (past + 1) * ROW_T, pl.ds(start + tile * ROW_T, ROW_T)],
                        jnp.zeros((), hist_ref.dtype),
                    )
                    for past in range(past_loc)
                ],
                0,
            )
        )
    masked = jnp.concatenate(columns, 1)
    term = jnp.dot(sigma[...], masked, preferred_element_type=jnp.float32)
    for tile in range(tiles):
        top = term[:ROW_T, tile * ROW_T : (tile + 1) * ROW_T]
        bottom = term[ROW_T:, tile * ROW_T : (tile + 1) * ROW_T]
        even, odd = unpack_pair(top, bottom)
        out_ref[(step * tiles + tile) * 2] = even.astype(out_ref.dtype)
        out_ref[(step * tiles + tile) * 2 + 1] = odd.astype(out_ref.dtype)


def memory_kernel(block, first_half, from_pieces, reach_ref, sigma_ref, hist_ref, out_ref, *scratch):
    own = lax.axis_index("c")
    half = 1 - own if first_half else own
    if from_pieces:
        sigma = scratch[0]
        for pair in range(sigma_ref.shape[0] // 2):
            top, bottom = unpack_pair(
                sigma_ref[2 * pair].astype(jnp.float32), sigma_ref[2 * pair + 1].astype(jnp.float32)
            )
            sigma[:ROW_T, pair * ROW_T : (pair + 1) * ROW_T] = top.astype(jnp.bfloat16)
            sigma[ROW_T:, pair * ROW_T : (pair + 1) * ROW_T] = bottom.astype(jnp.bfloat16)
    else:
        sigma = sigma_ref
    for step in range(hist_ref.shape[1] // 2 // TILE):
        column_tile(block, half, step, reach_ref, sigma, hist_ref, out_ref)


def first_kernel(reach_hbm, sigma_hbm, hist_hbm, out_ref, hist_ref, sigma_ref, reach_ref, sems):
    steps = hist_hbm.shape[1] // 2 // TILE
    own = lax.axis_index("c")
    copies = [
        pltpu.make_async_copy(reach_hbm, reach_ref, sems.at[0]),
        pltpu.make_async_copy(sigma_hbm, sigma_ref, sems.at[1]),
    ]
    for half in (1 - own, own):
        for step in range(steps):
            part = pl.ds(pl.multiple_of((half * steps + step) * TILE, TILE), TILE)
            copies.append(
                pltpu.make_async_copy(hist_hbm.at[:, part], hist_ref.at[:, part], sems.at[len(copies)])
            )
    for copy in copies:
        copy.start()
    copies[0].wait()
    copies[1].wait()
    for step in range(steps):
        copies[2 + step].wait()
        column_tile(0, 1 - own, step, reach_ref, sigma_ref, hist_ref, out_ref)
    for step in range(steps):
        copies[2 + steps + step].wait()


def first_terms(reach, sigma, history):
    rows, cols = history.shape
    there = pl.BlockSpec(memory_space=pltpu.HBM)
    return pl.pallas_call(
        first_kernel,
        out_shape=(
            jax.ShapeDtypeStruct((cols // 2 // HALF, ROW_T, ROW_T), jnp.bfloat16),
            jax.ShapeDtypeStruct(history.shape, history.dtype),
        ),
        in_specs=[there, there, there],
        out_specs=(VMEM, VMEM),
        scratch_shapes=[
            pltpu.VMEM(sigma.shape, sigma.dtype),
            pltpu.SMEM(reach.shape, reach.dtype),
            pltpu.SemaphoreType.DMA((2 + cols // TILE,)),
        ],
        cost_estimate=pl.CostEstimate(
            flops=2 * 256 * rows * cols // 2, bytes_accessed=2 * rows * cols + 1024 * 1024, transcendentals=0
        ),
        compiler_params=PARAMS,
        name="memory_first",
    )(reach, sigma, history)


def memory_terms(block, first_half, reach, sigma, history):
    rows, cols = history.shape
    from_pieces = sigma.ndim == 3
    return pl.pallas_call(
        functools.partial(memory_kernel, block, first_half, from_pieces),
        out_shape=jax.ShapeDtypeStruct((cols // 2 // HALF, ROW_T, ROW_T), jnp.bfloat16),
        in_specs=[SMEM, VMEM, VMEM],
        out_specs=VMEM,
        scratch_shapes=[pltpu.VMEM((2 * ROW_T, rows), jnp.bfloat16)] if from_pieces else [],
        cost_estimate=pl.CostEstimate(
            flops=2 * 256 * rows * cols // 2, bytes_accessed=rows * cols + 1024 * 1024, transcendentals=0
        ),
        compiler_params=PARAMS,
        name=f"memory_{block}_{int(first_half)}",
    )(reach, sigma, history)


def step_kernel(first, last, terms_ref, green_ref, step_ref, coupling_ref, *outs):
    integral = terms_ref[0].astype(jnp.float32)
    for piece in range(1, terms_ref.shape[0]):
        integral = integral + terms_ref[piece].astype(jnp.float32)
    low = low_lanes(integral.shape)
    if first:
        place = lax.axis_index(PLANE)
        tile = pl.multiple_of((lax.axis_index("c") * 8 + place // 2) * ROW_T, ROW_T)
        held = green_ref[:, pl.ds(tile, ROW_T)].astype(jnp.float32)
        before = jnp.where(place % 2 == 0, held, swap_halves(held))
    else:
        before = swap_halves(green_ref[...])
    source = integral + jnp.where(low, before, 0.0)
    dot = functools.partial(jnp.dot, precision=lax.Precision.HIGHEST, preferred_element_type=jnp.float32)
    moved = dot(step_ref[...], source)
    further = dot(step_ref[...], jnp.where(low, 0.0, swap_halves(moved)))
    rows = moved + further
    if last:
        piece = rows.astype(jnp.bfloat16)
    else:
        weights = jnp.broadcast_to(coupling_ref[...], rows.shape).T
        square = rows * rows
        piece = (weights * rows * square / (1.0 + square)).astype(jnp.bfloat16)
        outs[1][...] = rows
    for copy in range(outs[0].shape[0]):
        outs[0][copy] = piece


def advance(first, last, terms, green, step_inv, coupling):
    shapes = [jax.ShapeDtypeStruct((16 if last else 4, ROW_T, ROW_T), jnp.bfloat16)]
    if not last:
        shapes.append(jax.ShapeDtypeStruct((ROW_T, ROW_T), jnp.float32))
    out = pl.pallas_call(
        functools.partial(step_kernel, first, last),
        out_shape=tuple(shapes),
        in_specs=[VMEM, VMEM, VMEM, VMEM],
        out_specs=(VMEM,) * len(shapes),
        compiler_params=PARAMS,
        name=f"advance_{int(first)}{int(last)}",
    )(terms, green, step_inv, coupling)
    return out[0], (None if last else out[1])


def spread_kernel(own_ref, other_ref, out_ref):
    def write(ref, half):
        for pair in range(8):
            top, bottom = unpack_pair(ref[2 * pair].astype(jnp.float32), ref[2 * pair + 1].astype(jnp.float32))
            start = pl.multiple_of((half * 8 + pair) * ROW_T, ROW_T)
            out_ref[:ROW_T, pl.ds(start, ROW_T)] = top.astype(out_ref.dtype)
            out_ref[ROW_T:, pl.ds(start, ROW_T)] = bottom.astype(out_ref.dtype)

    core = lax.axis_index("c")
    write(own_ref, core)
    write(other_ref, 1 - core)


def spread_out(own, other):
    return pl.pallas_call(
        spread_kernel,
        out_shape=jax.ShapeDtypeStruct((2 * ROW_T, 16 * ROW_T), jnp.bfloat16),
        in_specs=[VMEM, VMEM],
        out_specs=VMEM,
        compiler_params=PARAMS,
        name="spread",
    )(own, other)


def exchange(x, axis):
    return lax.all_to_all(x, axis, 0, 0, tiled=True)


def local(history, self_rows, edge_rows, step_inv, coupling, reach):
    swap = [(0, 1), (1, 0)]
    weights = coupling[None, :]
    sigma, green, held = self_rows, edge_rows, history
    blocks = reach.shape[0]
    for block in range(blocks):
        last = block + 1 == blocks
        if block == 0:
            away, held = first_terms(reach, sigma, history)
        else:
            away = memory_terms(block, True, reach, sigma, held)
        arrived = lax.ppermute(away, "c", swap)
        kept = memory_terms(block, False, reach, sigma, held)
        pair = (kept.astype(jnp.float32) + arrived.astype(jnp.float32)).astype(jnp.bfloat16)
        terms = exchange(pair, PLANE)
        pieces, green = advance(block == 0, last, terms, green, step_inv, weights)
        if last:
            own = exchange(pieces, PLANE)
            return spread_out(own, lax.ppermute(own, "c", swap))
        distant = exchange(pieces, "far")
        around = jnp.broadcast_to(distant[None], (4, *distant.shape)).reshape(16, ROW_T, ROW_T)
        sigma = exchange(exchange(around, "near"), PLANE)


def solution(mesh):
    torus = Mesh(mesh.devices.reshape(4, 4, 2, 4, 4), ("x", "y", "c", "far", "near"))
    placed = (P(HIST, SECOND), P(None, HIST), P(None, SECOND), P(), P(), P())
    return jax.shard_map(local, mesh=torus, in_specs=placed, out_specs=P(None, SECOND), check_vma=False)
```

```python
import functools

import jax
import jax.numpy as jnp
from jax import lax
from jax.experimental import pallas as pl
from jax.experimental.pallas import tpu as pltpu
from jax.sharding import Mesh
from jax.sharding import PartitionSpec as P

HIST = ("x", "y_high", "y_low", "c")
PLANE = ("y_low", "x", "y_high")
SECOND = ("z_high", "z_low")
ROW_T = 128
HALF = 64
TILE = 256


def low_lanes(shape):
    return lax.broadcasted_iota(jnp.int32, shape, 1) < HALF


def swap_halves(value):
    return pltpu.roll(value, HALF, 1)


def unpack_pair(even, odd):
    low = low_lanes(even.shape)
    return (
        jnp.where(low, even, swap_halves(odd)),
        jnp.where(low, swap_halves(even), odd),
    )


VMEM = pl.BlockSpec(memory_space=pltpu.VMEM)
SMEM = pl.BlockSpec(memory_space=pltpu.SMEM)
PARAMS = pltpu.CompilerParams(vmem_limit_bytes=16 * 1024 * 1024)


def column_tile(block, half, step, reach_ref, sigma, hist_ref, out_ref):
    past_loc, tiles, steps = hist_ref.shape[0] // ROW_T, TILE // ROW_T, hist_ref.shape[1] // TILE
    tile_0 = (lax.axis_index(SECOND) * 2 + half) * steps * tiles + step * tiles
    columns = []
    for tile in range(tiles):
        live = reach_ref[block, tile_0 + tile] - lax.axis_index(HIST) * past_loc
        start = step * TILE + tile * ROW_T
        columns.append(
            jnp.concatenate(
                [
                    jnp.where(
                        past < live,
                        hist_ref[past * ROW_T : (past + 1) * ROW_T, start : start + ROW_T],
                        jnp.zeros((), hist_ref.dtype),
                    )
                    for past in range(past_loc)
                ],
                0,
            )
        )
    masked = jnp.concatenate(columns, 1)
    term = jnp.dot(sigma[...], masked, preferred_element_type=jnp.float32)
    for tile in range(tiles):
        top = term[:ROW_T, tile * ROW_T : (tile + 1) * ROW_T]
        bottom = term[ROW_T:, tile * ROW_T : (tile + 1) * ROW_T]
        even, odd = unpack_pair(top, bottom)
        out_ref[(step * tiles + tile) * 2] = even.astype(out_ref.dtype)
        out_ref[(step * tiles + tile) * 2 + 1] = odd.astype(out_ref.dtype)


def away_kernel(block, reach_in, sigma_in, hist_hbm, out_ref, kept_ref, sigma_out, away_ref, reach_own, sems):
    width = hist_hbm.shape[1] // 2
    steps = width // TILE
    own = lax.axis_index("c")
    copies = []
    for half, buffer in ((1 - own, away_ref), (own, kept_ref)):
        for step in range(steps):
            there = hist_hbm.at[:, pl.ds(pl.multiple_of(half * width + step * TILE, TILE), TILE)]
            here = buffer.at[:, step * TILE : (step + 1) * TILE]
            copies.append(pltpu.make_async_copy(there, here, sems.at[len(copies)]))
    if block == 0:
        inputs = [
            pltpu.make_async_copy(reach_in, reach_own, sems.at[2 * steps]),
            pltpu.make_async_copy(sigma_in, sigma_out, sems.at[2 * steps + 1]),
        ]
        for copy in inputs:
            copy.start()
    for copy in copies:
        copy.start()
    if block == 0:
        for copy in inputs:
            copy.wait()
        reach_ref = reach_own
    else:
        reach_ref = reach_in
        for pair in range(sigma_in.shape[0] // 2):
            top, bottom = unpack_pair(sigma_in[2 * pair].astype(jnp.float32), sigma_in[2 * pair + 1].astype(jnp.float32))
            sigma_out[:ROW_T, pair * ROW_T : (pair + 1) * ROW_T] = top.astype(jnp.bfloat16)
            sigma_out[ROW_T:, pair * ROW_T : (pair + 1) * ROW_T] = bottom.astype(jnp.bfloat16)
    for step in range(steps):
        copies[step].wait()
        column_tile(block, 1 - own, step, reach_ref, sigma_out, away_ref, out_ref)
    for step in range(steps):
        copies[steps + step].wait()


def own_kernel(block, reach_ref, sigma_ref, hist_ref, out_ref):
    for step in range(hist_ref.shape[1] // TILE):
        column_tile(block, lax.axis_index("c"), step, reach_ref, sigma_ref, hist_ref, out_ref)


def product_cost(rows, cols):
    return pl.CostEstimate(flops=512 * rows * cols, bytes_accessed=4 * rows * cols, transcendentals=0)


def away_terms(block, reach, sigma, history):
    rows, cols = history.shape
    hbm = pl.BlockSpec(memory_space=pltpu.HBM)
    history = pltpu.with_memory_space_constraint(history, pltpu.HBM)
    if block == 0:
        reach, sigma = (pltpu.with_memory_space_constraint(value, pltpu.HBM) for value in (reach, sigma))
    return pl.pallas_call(
        functools.partial(away_kernel, block),
        out_shape=(
            jax.ShapeDtypeStruct((cols // 2 // HALF, ROW_T, ROW_T), jnp.bfloat16),
            jax.ShapeDtypeStruct((rows, cols // 2), history.dtype),
            jax.ShapeDtypeStruct((2 * ROW_T, rows), jnp.bfloat16),
        ),
        in_specs=[hbm, hbm, hbm] if block == 0 else [SMEM, VMEM, hbm],
        out_specs=(VMEM, VMEM, VMEM),
        scratch_shapes=[
            pltpu.VMEM((rows, cols // 2), history.dtype),
            pltpu.SMEM(reach.shape, reach.dtype),
            pltpu.SemaphoreType.DMA((2 + cols // TILE,)),
        ],
        cost_estimate=product_cost(rows, cols // 2),
        compiler_params=PARAMS,
        name=f"away_{block}",
    )(reach, sigma, history)


def own_terms(block, reach, sigma, kept):
    return pl.pallas_call(
        functools.partial(own_kernel, block),
        out_shape=jax.ShapeDtypeStruct((kept.shape[1] // HALF, ROW_T, ROW_T), jnp.bfloat16),
        in_specs=[SMEM, VMEM, VMEM],
        out_specs=VMEM,
        cost_estimate=product_cost(*kept.shape),
        compiler_params=PARAMS,
        name=f"own_{block}",
    )(reach, sigma, kept)


def step_kernel(first, last, terms_ref, green_ref, step_ref, coupling_ref, *outs):
    integral = terms_ref[0].astype(jnp.float32)
    for piece in range(1, terms_ref.shape[0]):
        integral = integral + terms_ref[piece].astype(jnp.float32)
    low = low_lanes(integral.shape)
    if first:
        place = lax.axis_index(PLANE)
        tile = pl.multiple_of((lax.axis_index("c") * 8 + place // 2) * ROW_T, ROW_T)
        held = green_ref[:, pl.ds(tile, ROW_T)].astype(jnp.float32)
        before = jnp.where(place % 2 == 0, held, swap_halves(held))
    else:
        before = swap_halves(green_ref[...])
    source = integral + jnp.where(low, before, 0.0)
    dot = functools.partial(jnp.dot, precision=lax.Precision.HIGHEST, preferred_element_type=jnp.float32)
    moved = dot(step_ref[...], source)
    further = dot(step_ref[...], jnp.where(low, 0.0, swap_halves(moved)))
    rows = moved + further
    if last:
        piece = rows.astype(jnp.bfloat16)
    else:
        weights = jnp.broadcast_to(coupling_ref[...], rows.shape).T
        square = rows * rows
        piece = (weights * rows * square / (1.0 + square)).astype(jnp.bfloat16)
        outs[1][...] = rows
    for copy in range(outs[0].shape[0]):
        outs[0][copy] = piece


def advance(first, last, terms, green, step_inv, coupling):
    shapes = [jax.ShapeDtypeStruct((16 if last else 8, ROW_T, ROW_T), jnp.bfloat16)]
    if not last:
        shapes.append(jax.ShapeDtypeStruct((ROW_T, ROW_T), jnp.float32))
    out = pl.pallas_call(
        functools.partial(step_kernel, first, last),
        out_shape=tuple(shapes),
        in_specs=[VMEM, VMEM, VMEM, VMEM],
        out_specs=(VMEM,) * len(shapes),
        compiler_params=PARAMS,
        name=f"advance_{int(first)}{int(last)}",
    )(terms, green, step_inv, coupling)
    return out[0], (None if last else out[1])


def spread_kernel(own_ref, other_ref, out_ref):
    def write(ref, half):
        for pair in range(8):
            top, bottom = unpack_pair(ref[2 * pair].astype(jnp.float32), ref[2 * pair + 1].astype(jnp.float32))
            start = pl.multiple_of((half * 8 + pair) * ROW_T, ROW_T)
            out_ref[:ROW_T, pl.ds(start, ROW_T)] = top.astype(out_ref.dtype)
            out_ref[ROW_T:, pl.ds(start, ROW_T)] = bottom.astype(out_ref.dtype)

    core = lax.axis_index("c")
    write(own_ref, core)
    write(other_ref, 1 - core)


def spread_out(own, other):
    return pl.pallas_call(
        spread_kernel,
        out_shape=jax.ShapeDtypeStruct((2 * ROW_T, 16 * ROW_T), jnp.bfloat16),
        in_specs=[VMEM, VMEM],
        out_specs=VMEM,
        compiler_params=PARAMS,
        name="spread",
    )(own, other)


def exchange(x, axis):
    return lax.all_to_all(x, axis, 0, 0, tiled=True)


def gathered_over_second(copies):
    size = lax.axis_size(SECOND)
    ring = [(place, (place + 1) % size) for place in range(size)]
    mine = exchange(copies, "z_high")
    below = lax.ppermute(mine[: size // 4], SECOND, ring)
    above = lax.ppermute(mine[size // 4 :], SECOND, [(there, here) for here, there in ring])
    even = lax.axis_index("z_low") == 0
    return jnp.where(even, jnp.concatenate([mine, below, above]), jnp.concatenate([below, above, mine]))


def local(history, self_rows, edge_rows, step_inv, coupling, reach):
    swap = [(0, 1), (1, 0)]
    weights = coupling[None, :]
    sigma, green = self_rows, edge_rows
    blocks = reach.shape[0]
    for block in range(blocks):
        last = block + 1 == blocks
        away, kept, rows = away_terms(block, reach, sigma, history)
        arrived = lax.ppermute(away, "c", swap)
        mine = own_terms(block, reach, rows, kept)
        pair = (mine.astype(jnp.float32) + arrived.astype(jnp.float32)).astype(jnp.bfloat16)
        terms = exchange(pair, PLANE)
        pieces, green = advance(block == 0, last, terms, green, step_inv, weights)
        if last:
            own = exchange(pieces, PLANE)
            return spread_out(own, lax.ppermute(own, "c", swap))
        sigma = exchange(gathered_over_second(pieces), PLANE)


def solution(mesh):
    torus = Mesh(mesh.devices.reshape(4, 2, 2, 2, 8, 2), HIST + SECOND)
    placed = (P(HIST, SECOND), P(None, HIST), P(None, SECOND), P(), P(), P())
    return jax.shard_map(local, mesh=torus, in_specs=placed, out_specs=P(None, SECOND), check_vma=False)
```

```python
import functools

import jax
import jax.numpy as jnp
from jax import lax
from jax.experimental import pallas as pl
from jax.experimental.pallas import tpu as pltpu
from jax.sharding import Mesh
from jax.sharding import PartitionSpec as P

HIST = ("x", "y", "c")
SECOND = ("z_high", "z_low")
MIX = ("z_low", "x", "y")
ROW_T = 128
HALF = 64
QUARTER = 32
TILE = 256

VMEM = pl.BlockSpec(memory_space=pltpu.VMEM)
SMEM = pl.BlockSpec(memory_space=pltpu.SMEM)
PARAMS = pltpu.CompilerParams(vmem_limit_bytes=16 * 1024 * 1024)


def lower_lanes(shape, width):
    return (lax.broadcasted_iota(jnp.int32, shape, 1) // width) % 2 == 0


def swapped(first, second, width):
    low = lower_lanes(first.shape, width)
    return (
        jnp.where(low, first, pltpu.roll(second, width, 1)),
        jnp.where(low, pltpu.roll(first, ROW_T - width, 1), second),
    )


def lane_blocks_transposed(tiles):
    a0, a2 = swapped(tiles[0], tiles[2], HALF)
    a1, a3 = swapped(tiles[1], tiles[3], HALF)
    return (*swapped(a0, a1, QUARTER), *swapped(a2, a3, QUARTER))


PLACES = (0, ROW_T, HALF, ROW_T + HALF)


def tile_from_pieces(ref, group):
    return lane_blocks_transposed([ref[4 * group + piece].astype(jnp.float32) for piece in range(4)])


def column_tile(block, half, step, reach_ref, sigma, hist_ref, out_ref, edge_ref=None):
    past_loc, tiles = hist_ref.shape[0] // ROW_T, TILE // ROW_T
    steps = hist_ref.shape[1] // 2 // TILE
    start = pl.multiple_of((half * steps + step) * TILE, TILE)
    tile_0 = (lax.axis_index(SECOND) * 2 * steps + half * steps + step) * tiles
    columns = []
    for tile in range(tiles):
        live = reach_ref[block, tile_0 + tile] - lax.axis_index(HIST) * past_loc
        columns.append(
            jnp.concatenate(
                [
                    jnp.where(
                        past < live,
                        hist_ref[past * ROW_T : (past + 1) * ROW_T, pl.ds(start + tile * ROW_T, ROW_T)],
                        jnp.zeros((), hist_ref.dtype),
                    )
                    for past in range(past_loc)
                ],
                0,
            )
        )
    masked = jnp.concatenate(columns, 1)
    term = jnp.dot(sigma[...], masked, preferred_element_type=jnp.float32)
    for tile in range(tiles):
        parts = [term[at : at + HALF, tile * ROW_T : (tile + 1) * ROW_T] for at in PLACES]
        if edge_ref is not None:
            adds = lax.axis_index(("x", "y")) == 0
            for part in (0, 2):
                edge = edge_ref[PLACES[part] : PLACES[part] + HALF, pl.ds(start + tile * ROW_T, ROW_T)]
                parts[part] = parts[part] + jnp.where(adds, edge.astype(jnp.float32), 0.0)
        for piece, value in enumerate(lane_blocks_transposed(parts)):
            out_ref[(step * tiles + tile) * 4 + piece] = value.astype(out_ref.dtype)


def memory_kernel(block, first_half, from_pieces, with_edge, reach_ref, sigma_ref, hist_ref, *rest):
    own = lax.axis_index("c")
    half = 1 - own if first_half else own
    edge_ref = rest[0] if with_edge else None
    out_ref = rest[1] if with_edge else rest[0]
    sigma = sigma_ref
    if from_pieces:
        sigma = rest[-1]
        for group in range(sigma_ref.shape[0] // 4):
            for at, value in zip(PLACES, tile_from_pieces(sigma_ref, group)):
                sigma[at : at + HALF, group * ROW_T : (group + 1) * ROW_T] = value.astype(sigma.dtype)
    for step in range(hist_ref.shape[1] // 2 // TILE):
        column_tile(block, half, step, reach_ref, sigma, hist_ref, out_ref, edge_ref)


def product_cost(rows, cols):
    return pl.CostEstimate(flops=512 * rows * cols, bytes_accessed=4 * rows * cols, transcendentals=0)


def pieces_shape(cols):
    return jax.ShapeDtypeStruct((cols // QUARTER, HALF, ROW_T), jnp.bfloat16)


def memory_terms(block, first_half, reach, sigma, history, edge=None):
    rows, cols = history.shape
    from_pieces = sigma.ndim == 3
    extra = () if edge is None else (edge,)
    return pl.pallas_call(
        functools.partial(memory_kernel, block, first_half, from_pieces, edge is not None),
        out_shape=pieces_shape(cols // 2),
        in_specs=[SMEM, VMEM, VMEM] + [VMEM] * len(extra),
        out_specs=VMEM,
        scratch_shapes=[pltpu.VMEM((2 * ROW_T, rows), jnp.bfloat16)] if from_pieces else [],
        cost_estimate=product_cost(rows, cols // 2),
        compiler_params=PARAMS,
        name=f"memory_{block}_{int(first_half)}",
    )(reach, sigma, history, *extra)


def first_kernel(reach_hbm, sigma_hbm, hist_hbm, out_ref, hist_ref, sigma_ref, reach_ref, sems):
    steps = hist_hbm.shape[1] // 2 // TILE
    own = lax.axis_index("c")
    copies = [
        pltpu.make_async_copy(reach_hbm, reach_ref, sems.at[0]),
        pltpu.make_async_copy(sigma_hbm, sigma_ref, sems.at[1]),
    ]
    for half in (1 - own, own):
        for step in range(steps):
            part = pl.ds(pl.multiple_of((half * steps + step) * TILE, TILE), TILE)
            copies.append(
                pltpu.make_async_copy(hist_hbm.at[:, part], hist_ref.at[:, part], sems.at[len(copies)])
            )
    for copy in copies:
        copy.start()
    copies[0].wait()
    copies[1].wait()
    for step in range(steps):
        copies[2 + step].wait()
        column_tile(0, 1 - own, step, reach_ref, sigma_ref, hist_ref, out_ref)
    for step in range(steps):
        copies[2 + steps + step].wait()


def first_terms(reach, sigma, history):
    rows, cols = history.shape
    there = pl.BlockSpec(memory_space=pltpu.HBM)
    return pl.pallas_call(
        first_kernel,
        out_shape=(
            pieces_shape(cols // 2),
            jax.ShapeDtypeStruct(history.shape, history.dtype),
            jax.ShapeDtypeStruct(sigma.shape, sigma.dtype),
        ),
        in_specs=[there, there, there],
        out_specs=(VMEM, VMEM, VMEM),
        scratch_shapes=[
            pltpu.SMEM(reach.shape, reach.dtype),
            pltpu.SemaphoreType.DMA((2 + cols // TILE,)),
        ],
        cost_estimate=product_cost(rows, cols // 2),
        compiler_params=PARAMS,
        name="memory_first",
    )(*(pltpu.with_memory_space_constraint(value, pltpu.HBM) for value in (reach, sigma, history)))


def step_kernel(first, last, terms_ref, step_ref, coupling_ref, *refs):
    count = terms_ref.shape[0] // 2
    sums = []
    for plane in range(2):
        total = terms_ref[plane * count].astype(jnp.float32)
        for place in range(1, count):
            total = total + terms_ref[plane * count + place].astype(jnp.float32)
        sums.append(total)
    source = jnp.concatenate(swapped(*sums, HALF), 0)
    step_0 = lower_lanes(source.shape, QUARTER)
    outs = refs
    if not first:
        source = source + jnp.where(step_0, pltpu.roll(refs[0][...], ROW_T - QUARTER, 1), 0.0)
        outs = refs[1:]
    dot = functools.partial(jnp.dot, precision=lax.Precision.HIGHEST, preferred_element_type=jnp.float32)
    moved = dot(step_ref[...], source)
    rows = moved + dot(step_ref[...], jnp.where(step_0, 0.0, pltpu.roll(moved, QUARTER, 1)))
    result = rows
    if not last:
        weights = jnp.broadcast_to(coupling_ref[...], rows.shape).T
        square = rows * rows
        result = weights * rows * square / (1.0 + square)
        outs[1][...] = rows
    planes = [value.astype(jnp.bfloat16) for value in swapped(result[:HALF], result[HALF:], HALF)]
    for plane in range(2):
        for copy in range(outs[0].shape[1 if last else 0]):
            if last:
                outs[0][plane, copy] = planes[plane]
            else:
                outs[0][copy, plane] = planes[plane]


def advance(first, last, terms, green, step_inv, coupling):
    copies = (2, 16) if last else (8, 2)
    shapes = [jax.ShapeDtypeStruct((*copies, HALF, ROW_T), jnp.bfloat16)]
    if not last:
        shapes.append(jax.ShapeDtypeStruct((ROW_T, ROW_T), jnp.float32))
    args = (terms, step_inv, coupling) + (() if first else (green,))
    out = pl.pallas_call(
        functools.partial(step_kernel, first, last),
        out_shape=tuple(shapes),
        in_specs=[VMEM] * len(args),
        out_specs=(VMEM,) * len(shapes),
        compiler_params=PARAMS,
        name=f"advance_{int(first)}{int(last)}",
    )(*args)
    return out[0], (None if last else out[1])


def spread_kernel(own_ref, other_ref, out_ref):
    core = lax.axis_index("c")
    for ref, half in ((own_ref, core), (other_ref, 1 - core)):
        groups = ref.shape[0] // 4
        for group in range(groups):
            part = pl.ds(pl.multiple_of((half * groups + group) * ROW_T, ROW_T), ROW_T)
            for at, value in zip(PLACES, tile_from_pieces(ref, group)):
                out_ref[at : at + HALF, part] = value.astype(out_ref.dtype)


def spread_out(own, other):
    return pl.pallas_call(
        spread_kernel,
        out_shape=jax.ShapeDtypeStruct((2 * ROW_T, 2 * own.shape[0] * QUARTER), jnp.bfloat16),
        in_specs=[VMEM, VMEM],
        out_specs=VMEM,
        compiler_params=PARAMS,
        name="spread",
    )(own, other)


def exchange(x, axis):
    return lax.all_to_all(x, axis, 0, 0, tiled=True)


def local(history, self_rows, edge_rows, step_inv, coupling, reach):
    swap = [(0, 1), (1, 0)]
    weights = coupling[None, :]
    green, blocks = None, reach.shape[0]
    for block in range(blocks):
        last = block + 1 == blocks
        if block == 0:
            away, held, rows = first_terms(reach, self_rows, history)
        else:
            away = memory_terms(block, True, reach, rows, held)
        arrived = lax.ppermute(away, "c", swap)
        mine = memory_terms(block, False, reach, rows, held, edge_rows if block == 0 else None)
        pair = (mine.astype(jnp.float32) + arrived.astype(jnp.float32)).astype(jnp.bfloat16)
        terms = exchange(pair, MIX)
        pieces, green = advance(block == 0, last, terms, green, step_inv, weights)
        if last:
            own = exchange(pieces.reshape(-1, HALF, ROW_T), MIX)
            return spread_out(own, lax.ppermute(own, "c", swap))
        places = exchange(pieces, "z_high").reshape(16, HALF, ROW_T)
        rows = exchange(jnp.concatenate([places, places]), MIX)


def solution(mesh):
    torus = Mesh(mesh.devices.reshape(4, 4, 2, 8, 2), HIST + SECOND)
    placed = (P(HIST, SECOND), P(None, HIST), P(None, SECOND), P(), P(), P())
    return jax.shard_map(local, mesh=torus, in_specs=placed, out_specs=P(None, SECOND), check_vma=False)
```

```python
import functools

import jax
import jax.numpy as jnp
from jax import lax
from jax.experimental import pallas as pl
from jax.experimental.pallas import tpu as pltpu
from jax.sharding import Mesh
from jax.sharding import PartitionSpec as P

HIST = ("x_high", "x_low", "y_high", "y_low", "c")
SECOND = ("z_3", "z_2", "z_1", "z_0")
FAR = ("z_3", "z_1", "z_2")
MIX = ("z_0", "x_high", "y_high", "x_low", "y_low")
ROW_T = 128
HALF = 64
QUARTER = 32
TILE = 512

VMEM = pl.BlockSpec(memory_space=pltpu.VMEM)
SMEM = pl.BlockSpec(memory_space=pltpu.SMEM)
PARAMS = pltpu.CompilerParams(vmem_limit_bytes=16 * 1024 * 1024)


def lower_lanes(shape, width):
    return (lax.broadcasted_iota(jnp.int32, shape, 1) // width) % 2 == 0


def swapped(first, second, width):
    low = lower_lanes(first.shape, width)
    return (
        jnp.where(low, first, pltpu.roll(second, width, 1)),
        jnp.where(low, pltpu.roll(first, ROW_T - width, 1), second),
    )


def lane_blocks_transposed(tiles):
    a0, a2 = swapped(tiles[0], tiles[2], HALF)
    a1, a3 = swapped(tiles[1], tiles[3], HALF)
    return (*swapped(a0, a1, QUARTER), *swapped(a2, a3, QUARTER))


PLACES = (0, ROW_T, HALF, ROW_T + HALF)


def tile_from_pieces(ref, group):
    return lane_blocks_transposed([ref[4 * group + piece] for piece in range(4)])


def column_tile(block, half, step, reach_ref, sigma, hist_ref, out_ref, edge_ref=None):
    past_loc, tiles = hist_ref.shape[0] // ROW_T, TILE // ROW_T
    steps = hist_ref.shape[1] // 2 // TILE
    start = pl.multiple_of((half * steps + step) * TILE, TILE)
    tile_0 = (lax.axis_index(SECOND) * 2 * steps + half * steps + step) * tiles
    columns = []
    for tile in range(tiles):
        live = reach_ref[block, tile_0 + tile] - lax.axis_index(HIST) * past_loc
        parts = []
        for past in range(past_loc):
            keep = jnp.full((1, ROW_T), jnp.where(past < live, 1.0, 0.0), jnp.float32).astype(hist_ref.dtype)
            part = hist_ref[past * ROW_T : (past + 1) * ROW_T, pl.ds(start + tile * ROW_T, ROW_T)]
            parts.append(part * keep)
        columns.append(jnp.concatenate(parts, 0))
    masked = jnp.concatenate(columns, 1)
    term = jnp.dot(sigma[...], masked, preferred_element_type=jnp.float32)
    for tile in range(tiles):
        parts = [term[at : at + HALF, tile * ROW_T : (tile + 1) * ROW_T] for at in PLACES]
        if edge_ref is not None:
            adds = lax.axis_index(HIST[:4]) == 0
            for part in (0, 2):
                edge = edge_ref[PLACES[part] : PLACES[part] + HALF, pl.ds(start + tile * ROW_T, ROW_T)]
                parts[part] = parts[part] + jnp.where(adds, edge.astype(jnp.float32), 0.0)
        for piece, value in enumerate(lane_blocks_transposed([part.astype(out_ref.dtype) for part in parts])):
            out_ref[(step * tiles + tile) * 4 + piece] = value.astype(out_ref.dtype)


def memory_kernel(block, first_half, with_edge, reach_ref, sigma_ref, hist_ref, *rest):
    own = lax.axis_index("c")
    half = 1 - own if first_half else own
    edge_ref, outs = (rest[0], rest[1:]) if with_edge else (None, rest)
    sigma = sigma_ref
    if first_half:
        sigma = outs[1]
        for group in range(sigma_ref.shape[0] // 4):
            for at, value in zip(PLACES, tile_from_pieces(sigma_ref, group)):
                sigma[at : at + HALF, group * ROW_T : (group + 1) * ROW_T] = value.astype(sigma.dtype)
    for step in range(hist_ref.shape[1] // 2 // TILE):
        column_tile(block, half, step, reach_ref, sigma, hist_ref, outs[0], edge_ref)


def product_cost(rows, cols):
    return pl.CostEstimate(flops=512 * rows * cols, bytes_accessed=4 * rows * cols, transcendentals=0)


def pieces_shape(cols):
    return jax.ShapeDtypeStruct((cols // QUARTER, HALF, ROW_T), jnp.bfloat16)


def memory_terms(block, first_half, reach, sigma, history, edge=None):
    rows, cols = history.shape
    extra = () if edge is None else (edge,)
    joined = (jax.ShapeDtypeStruct((2 * ROW_T, rows), jnp.bfloat16),) if first_half else ()
    return pl.pallas_call(
        functools.partial(memory_kernel, block, first_half, edge is not None),
        out_shape=(pieces_shape(cols // 2), *joined),
        in_specs=[SMEM, VMEM, VMEM] + [VMEM] * len(extra),
        out_specs=(VMEM,) * (1 + len(joined)),
        cost_estimate=product_cost(rows, cols // 2),
        compiler_params=PARAMS,
        name=f"memory_{block}_{int(first_half)}",
    )(reach, sigma, history, *extra)


def first_kernel(reach_hbm, sigma_hbm, hist_hbm, out_ref, hist_ref, sigma_ref, reach_ref, sems):
    steps = hist_hbm.shape[1] // 2 // TILE
    own = lax.axis_index("c")
    copies = [
        pltpu.make_async_copy(reach_hbm, reach_ref, sems.at[0]),
        pltpu.make_async_copy(sigma_hbm, sigma_ref, sems.at[1]),
    ]
    for half in (1 - own, own):
        for step in range(steps):
            part = pl.ds(pl.multiple_of((half * steps + step) * TILE, TILE), TILE)
            copies.append(
                pltpu.make_async_copy(hist_hbm.at[:, part], hist_ref.at[:, part], sems.at[len(copies)])
            )
    for copy in copies:
        copy.start()
    copies[0].wait()
    copies[1].wait()
    for step in range(steps):
        copies[2 + step].wait()
        column_tile(0, 1 - own, step, reach_ref, sigma_ref, hist_ref, out_ref)
    for step in range(steps):
        copies[2 + steps + step].wait()


def first_terms(reach, sigma, history):
    rows, cols = history.shape
    there = pl.BlockSpec(memory_space=pltpu.HBM)
    return pl.pallas_call(
        first_kernel,
        out_shape=(
            pieces_shape(cols // 2),
            jax.ShapeDtypeStruct(history.shape, history.dtype),
            jax.ShapeDtypeStruct(sigma.shape, sigma.dtype),
        ),
        in_specs=[there, there, there],
        out_specs=(VMEM, VMEM, VMEM),
        scratch_shapes=[
            pltpu.SMEM(reach.shape, reach.dtype),
            pltpu.SemaphoreType.DMA((2 + cols // TILE,)),
        ],
        cost_estimate=product_cost(rows, cols // 2),
        compiler_params=PARAMS,
        name="memory_first",
    )(*(pltpu.with_memory_space_constraint(value, pltpu.HBM) for value in (reach, sigma, history)))


def step_kernel(first, last, terms_ref, step_ref, coupling_ref, *refs):
    count = terms_ref.shape[0] // 2
    sums = []
    for plane in range(2):
        total = terms_ref[plane * count].astype(jnp.float32)
        for place in range(1, count):
            total = total + terms_ref[plane * count + place].astype(jnp.float32)
        sums.append(total)
    source = jnp.concatenate(swapped(*sums, HALF), 0)
    step_0 = lower_lanes(source.shape, QUARTER)
    outs = refs
    if not first:
        source = source + jnp.where(step_0, pltpu.roll(refs[0][...], ROW_T - QUARTER, 1), 0.0)
        outs = refs[1:]
    dot = functools.partial(jnp.dot, precision=lax.Precision.HIGHEST, preferred_element_type=jnp.float32)
    moved = dot(step_ref[...], source)
    rows = moved + dot(step_ref[...], jnp.where(step_0, 0.0, pltpu.roll(moved, QUARTER, 1)))
    result = rows
    if not last:
        weights = jnp.broadcast_to(coupling_ref[...], rows.shape).T
        square = rows * rows
        result = weights * rows * square / (1.0 + square)
        outs[1][...] = rows
    planes = [value.astype(jnp.bfloat16) for value in swapped(result[:HALF], result[HALF:], HALF)]
    for plane in range(2):
        for copy in range(outs[0].shape[1 if last else 0]):
            if last:
                outs[0][plane, copy] = planes[plane]
            else:
                outs[0][copy, plane] = planes[plane]


def advance(first, last, terms, green, step_inv, coupling):
    copies = (2, 16) if last else (8, 2)
    shapes = [jax.ShapeDtypeStruct((*copies, HALF, ROW_T), jnp.bfloat16)]
    if not last:
        shapes.append(jax.ShapeDtypeStruct((ROW_T, ROW_T), jnp.float32))
    args = (terms, step_inv, coupling) + (() if first else (green,))
    out = pl.pallas_call(
        functools.partial(step_kernel, first, last),
        out_shape=tuple(shapes),
        in_specs=[VMEM] * len(args),
        out_specs=(VMEM,) * len(shapes),
        compiler_params=PARAMS,
        name=f"advance_{int(first)}{int(last)}",
    )(*args)
    return out[0], (None if last else out[1])


def spread_kernel(first, pieces_ref, *refs):
    out_hbm, tile_ref, sems = refs[-3:]
    core = lax.axis_index("c")
    half = core if first else 1 - core
    groups = pieces_ref.shape[0] // 4
    copies = []
    for group in range(groups):
        for at, value in zip(PLACES, tile_from_pieces(pieces_ref, group)):
            tile_ref[at : at + HALF, group * ROW_T : (group + 1) * ROW_T] = value.astype(tile_ref.dtype)
        if group % 2:
            here = tile_ref.at[:, (group - 1) * ROW_T : (group + 1) * ROW_T]
            start = pl.multiple_of((half * groups + group - 1) * ROW_T, 2 * ROW_T)
            copies.append(pltpu.make_async_copy(here, out_hbm.at[:, pl.ds(start, 2 * ROW_T)], sems.at[group // 2]))
            copies[-1].start()
    for copy in copies:
        copy.wait()


def spread_out(pieces, result=None):
    width = pieces.shape[0] * QUARTER
    first = result is None
    hbm = pl.BlockSpec(memory_space=pltpu.HBM)
    return pl.pallas_call(
        functools.partial(spread_kernel, first),
        out_shape=jax.ShapeDtypeStruct((2 * ROW_T, 2 * width), jnp.bfloat16),
        in_specs=[VMEM] if first else [VMEM, hbm],
        out_specs=hbm,
        scratch_shapes=[pltpu.VMEM((2 * ROW_T, width), jnp.bfloat16), pltpu.SemaphoreType.DMA((width // (2 * ROW_T),))],
        input_output_aliases={} if first else {1: 0},
        cost_estimate=pl.CostEstimate(flops=0, bytes_accessed=8 * ROW_T * width, transcendentals=0),
        compiler_params=PARAMS,
        name=f"spread_{int(first)}",
    )(*((pieces,) if first else (pieces, result)))


def exchange(x, axis):
    return lax.all_to_all(x, axis, 0, 0, tiled=True)


def local(history, self_rows, edge_rows, step_inv, coupling, reach):
    swap = [(0, 1), (1, 0)]
    weights = coupling[None, :]
    green, blocks = None, reach.shape[0]
    for block in range(blocks):
        last = block + 1 == blocks
        if block == 0:
            away, held, rows = first_terms(reach, self_rows, history)
        else:
            away, rows = memory_terms(block, True, reach, rows, held)
        arrived = lax.ppermute(away, "c", swap)
        (mine,) = memory_terms(block, False, reach, rows, held, edge_rows if block == 0 else None)
        pair = (mine.astype(jnp.float32) + arrived.astype(jnp.float32)).astype(jnp.bfloat16)
        terms = exchange(pair, MIX)
        pieces, green = advance(block == 0, last, terms, green, step_inv, weights)
        if last:
            own = exchange(pieces.reshape(-1, HALF, ROW_T), MIX)
            other = lax.ppermute(own, "c", swap)
            return spread_out(other, spread_out(own))
        places = exchange(pieces, FAR).reshape(16, HALF, ROW_T)
        rows = exchange(jnp.concatenate([places, places]), MIX)


def solution(mesh):
    torus = Mesh(mesh.devices.reshape((2,) * 9), HIST + SECOND)
    placed = (P(HIST, SECOND), P(None, HIST), P(None, SECOND), P(), P(), P())
    return jax.shard_map(local, mesh=torus, in_specs=placed, out_specs=P(None, SECOND), check_vma=False)
```

```python
import functools

import jax
import jax.numpy as jnp
from jax import lax
from jax.experimental import pallas as pl
from jax.experimental.pallas import tpu as pltpu
from jax.sharding import Mesh
from jax.sharding import PartitionSpec as P

HIST = ("x_high", "x_low", "y_high", "y_low", "c")
SECOND = ("z_3", "z_2", "z_1", "z_0")
FAR = ("z_1", "z_3", "z_2")
MIX = ("z_0", "y_high", "x_high", "x_low", "y_low")
ROW_T = 128
HALF = 64
QUARTER = 32
TILE = 512

VMEM = pl.BlockSpec(memory_space=pltpu.VMEM)
SMEM = pl.BlockSpec(memory_space=pltpu.SMEM)
PARAMS = pltpu.CompilerParams(vmem_limit_bytes=16 * 1024 * 1024)


def lower_lanes(shape, width):
    return (lax.broadcasted_iota(jnp.int32, shape, 1) // width) % 2 == 0


def swapped(first, second, width):
    low = lower_lanes(first.shape, width)
    return (
        jnp.where(low, first, pltpu.roll(second, width, 1)),
        jnp.where(low, pltpu.roll(first, ROW_T - width, 1), second),
    )


def lane_blocks_transposed(tiles):
    a0, a2 = swapped(tiles[0], tiles[2], HALF)
    a1, a3 = swapped(tiles[1], tiles[3], HALF)
    return (*swapped(a0, a1, QUARTER), *swapped(a2, a3, QUARTER))


PLACES = (0, ROW_T, HALF, ROW_T + HALF)


def tile_from_pieces(ref, group):
    return lane_blocks_transposed([ref[4 * group + piece] for piece in range(4)])


def column_tile(block, half, step, reach_ref, sigma, hist_ref, out_ref, edge_ref=None):
    past_loc, tiles = hist_ref.shape[0] // ROW_T, TILE // ROW_T
    steps = hist_ref.shape[1] // 2 // TILE
    start = pl.multiple_of((half * steps + step) * TILE, TILE)
    tile_0 = (lax.axis_index(SECOND) * 2 * steps + half * steps + step) * tiles
    columns = []
    for tile in range(tiles):
        live = reach_ref[block, tile_0 + tile] - lax.axis_index(HIST) * past_loc
        parts = []
        for past in range(past_loc):
            keep = jnp.full((1, ROW_T), jnp.where(past < live, 1.0, 0.0), jnp.float32).astype(hist_ref.dtype)
            part = hist_ref[past * ROW_T : (past + 1) * ROW_T, pl.ds(start + tile * ROW_T, ROW_T)]
            parts.append(part * keep)
        columns.append(jnp.concatenate(parts, 0))
    masked = jnp.concatenate(columns, 1)
    term = jnp.dot(sigma[...], masked, preferred_element_type=jnp.float32)
    for tile in range(tiles):
        parts = [term[at : at + HALF, tile * ROW_T : (tile + 1) * ROW_T] for at in PLACES]
        if edge_ref is not None:
            adds = lax.axis_index(HIST[:4]) == 0
            for part in (0, 2):
                edge = edge_ref[PLACES[part] : PLACES[part] + HALF, pl.ds(start + tile * ROW_T, ROW_T)]
                parts[part] = parts[part] + jnp.where(adds, edge.astype(jnp.float32), 0.0)
        for piece, value in enumerate(lane_blocks_transposed([part.astype(out_ref.dtype) for part in parts])):
            out_ref[(step * tiles + tile) * 4 + piece] = value.astype(out_ref.dtype)


def memory_kernel(block, first_half, with_edge, reach_ref, sigma_ref, hist_ref, *rest):
    own = lax.axis_index("c")
    half = 1 - own if first_half else own
    edge_ref, outs = (rest[0], rest[1:]) if with_edge else (None, rest)
    sigma = sigma_ref
    if first_half:
        sigma = outs[1]
        for group in range(sigma_ref.shape[0] // 4):
            for at, value in zip(PLACES, tile_from_pieces(sigma_ref, group)):
                sigma[at : at + HALF, group * ROW_T : (group + 1) * ROW_T] = value.astype(sigma.dtype)
    for step in range(hist_ref.shape[1] // 2 // TILE):
        column_tile(block, half, step, reach_ref, sigma, hist_ref, outs[0], edge_ref)


def product_cost(rows, cols):
    return pl.CostEstimate(flops=512 * rows * cols, bytes_accessed=4 * rows * cols, transcendentals=0)


def pieces_shape(cols):
    return jax.ShapeDtypeStruct((cols // QUARTER, HALF, ROW_T), jnp.bfloat16)


def memory_terms(block, first_half, reach, sigma, history, edge=None):
    rows, cols = history.shape
    extra = () if edge is None else (edge,)
    joined = (jax.ShapeDtypeStruct((2 * ROW_T, rows), jnp.bfloat16),) if first_half else ()
    return pl.pallas_call(
        functools.partial(memory_kernel, block, first_half, edge is not None),
        out_shape=(pieces_shape(cols // 2), *joined),
        in_specs=[SMEM, VMEM, VMEM] + [VMEM] * len(extra),
        out_specs=(VMEM,) * (1 + len(joined)),
        cost_estimate=product_cost(rows, cols // 2),
        compiler_params=PARAMS,
        name=f"memory_{block}_{int(first_half)}",
    )(reach, sigma, history, *extra)


def first_kernel(reach_hbm, sigma_hbm, hist_hbm, out_ref, hist_ref, sigma_ref, reach_ref, sems):
    steps = hist_hbm.shape[1] // 2 // TILE
    own = lax.axis_index("c")
    copies = [
        pltpu.make_async_copy(reach_hbm, reach_ref, sems.at[0]),
        pltpu.make_async_copy(sigma_hbm, sigma_ref, sems.at[1]),
    ]
    for half in (1 - own, own):
        for step in range(steps):
            part = pl.ds(pl.multiple_of((half * steps + step) * TILE, TILE), TILE)
            copies.append(
                pltpu.make_async_copy(hist_hbm.at[:, part], hist_ref.at[:, part], sems.at[len(copies)])
            )
    for copy in copies:
        copy.start()
    copies[0].wait()
    copies[1].wait()
    for step in range(steps):
        copies[2 + step].wait()
        column_tile(0, 1 - own, step, reach_ref, sigma_ref, hist_ref, out_ref)
    for step in range(steps):
        copies[2 + steps + step].wait()


def first_terms(reach, sigma, history):
    rows, cols = history.shape
    there = pl.BlockSpec(memory_space=pltpu.HBM)
    return pl.pallas_call(
        first_kernel,
        out_shape=(
            pieces_shape(cols // 2),
            jax.ShapeDtypeStruct(history.shape, history.dtype),
            jax.ShapeDtypeStruct(sigma.shape, sigma.dtype),
        ),
        in_specs=[there, there, there],
        out_specs=(VMEM, VMEM, VMEM),
        scratch_shapes=[
            pltpu.SMEM(reach.shape, reach.dtype),
            pltpu.SemaphoreType.DMA((2 + cols // TILE,)),
        ],
        cost_estimate=product_cost(rows, cols // 2),
        compiler_params=PARAMS,
        name="memory_first",
    )(*(pltpu.with_memory_space_constraint(value, pltpu.HBM) for value in (reach, sigma, history)))


def in_two(value):
    high = value.astype(jnp.bfloat16)
    return high, (value - high.astype(jnp.float32)).astype(jnp.bfloat16)


def product(left, value):
    right = in_two(value)
    dot = functools.partial(jnp.dot, preferred_element_type=jnp.float32)
    return dot(left[0], right[0]) + (dot(left[0], right[1]) + dot(left[1], right[0]))


def step_kernel(first, last, terms_ref, step_ref, coupling_ref, *refs):
    count = terms_ref.shape[0] // 2
    sums = []
    for plane in range(2):
        total = terms_ref[plane * count].astype(jnp.float32)
        for place in range(1, count):
            total = total + terms_ref[plane * count + place].astype(jnp.float32)
        sums.append(total)
    source = jnp.concatenate(swapped(*sums, HALF), 0)
    step_0 = lower_lanes(source.shape, QUARTER)
    outs = refs
    if not first:
        source = source + jnp.where(step_0, pltpu.roll(refs[0][...], ROW_T - QUARTER, 1), 0.0)
        outs = refs[1:]
    operator = in_two(step_ref[...])
    moved = product(operator, source)
    rows = moved + product(operator, jnp.where(step_0, 0.0, pltpu.roll(moved, QUARTER, 1)))
    result = rows
    if not last:
        weights = jnp.broadcast_to(coupling_ref[...], rows.shape).T
        square = rows * rows
        result = weights * rows * square / (1.0 + square)
        outs[1][...] = rows
    planes = [value.astype(jnp.bfloat16) for value in swapped(result[:HALF], result[HALF:], HALF)]
    for plane in range(2):
        for copy in range(outs[0].shape[1 if last else 0]):
            if last:
                outs[0][plane, copy] = planes[plane]
            else:
                outs[0][copy, plane] = planes[plane]


def advance(first, last, terms, green, step_inv, coupling):
    copies = (2, 16) if last else (8, 2)
    shapes = [jax.ShapeDtypeStruct((*copies, HALF, ROW_T), jnp.bfloat16)]
    if not last:
        shapes.append(jax.ShapeDtypeStruct((ROW_T, ROW_T), jnp.float32))
    args = (terms, step_inv, coupling) + (() if first else (green,))
    out = pl.pallas_call(
        functools.partial(step_kernel, first, last),
        out_shape=tuple(shapes),
        in_specs=[VMEM] * len(args),
        out_specs=(VMEM,) * len(shapes),
        compiler_params=PARAMS,
        name=f"advance_{int(first)}{int(last)}",
    )(*args)
    return out[0], (None if last else out[1])


def spread_kernel(first, pieces_ref, *refs):
    out_hbm, tile_ref, sems = refs[-3:]
    core = lax.axis_index("c")
    half = core if first else 1 - core
    groups = pieces_ref.shape[0] // 4
    copies = []
    for group in range(groups):
        for at, value in zip(PLACES, tile_from_pieces(pieces_ref, group)):
            tile_ref[at : at + HALF, group * ROW_T : (group + 1) * ROW_T] = value.astype(tile_ref.dtype)
        if group % 2:
            here = tile_ref.at[:, (group - 1) * ROW_T : (group + 1) * ROW_T]
            start = pl.multiple_of((half * groups + group - 1) * ROW_T, 2 * ROW_T)
            copies.append(pltpu.make_async_copy(here, out_hbm.at[:, pl.ds(start, 2 * ROW_T)], sems.at[group // 2]))
            copies[-1].start()
    for copy in copies:
        copy.wait()


def spread_out(pieces, result=None):
    width = pieces.shape[0] * QUARTER
    first = result is None
    hbm = pl.BlockSpec(memory_space=pltpu.HBM)
    return pl.pallas_call(
        functools.partial(spread_kernel, first),
        out_shape=jax.ShapeDtypeStruct((2 * ROW_T, 2 * width), jnp.bfloat16),
        in_specs=[VMEM] if first else [VMEM, hbm],
        out_specs=hbm,
        scratch_shapes=[pltpu.VMEM((2 * ROW_T, width), jnp.bfloat16), pltpu.SemaphoreType.DMA((width // (2 * ROW_T),))],
        input_output_aliases={} if first else {1: 0},
        cost_estimate=pl.CostEstimate(flops=0, bytes_accessed=8 * ROW_T * width, transcendentals=0),
        compiler_params=PARAMS,
        name=f"spread_{int(first)}",
    )(*((pieces,) if first else (pieces, result)))


def exchange(x, axis):
    return lax.all_to_all(x, axis, 0, 0, tiled=True)


def local(history, self_rows, edge_rows, step_inv, coupling, reach):
    swap = [(0, 1), (1, 0)]
    weights = coupling[None, :]
    green, blocks = None, reach.shape[0]
    for block in range(blocks):
        last = block + 1 == blocks
        if block == 0:
            away, held, rows = first_terms(reach, self_rows, history)
        else:
            away, rows = memory_terms(block, True, reach, rows, held)
        arrived = lax.ppermute(away, "c", swap)
        (mine,) = memory_terms(block, False, reach, rows, held, edge_rows if block == 0 else None)
        pair = (mine.astype(jnp.float32) + arrived.astype(jnp.float32)).astype(jnp.bfloat16)
        terms = exchange(pair, MIX)
        pieces, green = advance(block == 0, last, terms, green, step_inv, weights)
        if last:
            own = exchange(pieces.reshape(-1, HALF, ROW_T), MIX)
            other = lax.ppermute(own, "c", swap)
            return spread_out(other, spread_out(own))
        places = exchange(pieces, FAR).reshape(16, HALF, ROW_T)
        rows = exchange(jnp.concatenate([places, places]), MIX)


def solution(mesh):
    torus = Mesh(mesh.devices.reshape((2,) * 9), HIST + SECOND)
    placed = (P(HIST, SECOND), P(None, HIST), P(None, SECOND), P(), P(), P())
    return jax.shard_map(local, mesh=torus, in_specs=placed, out_specs=P(None, SECOND), check_vma=False)
```

```python
import functools

import jax
import jax.numpy as jnp
from jax import lax
from jax.experimental import pallas as pl
from jax.experimental.pallas import tpu as pltpu
from jax.sharding import Mesh
from jax.sharding import PartitionSpec as P

HIST = ("x_high", "x_low", "y_high", "y_low", "c")
SECOND = ("z_3", "z_2", "z_1", "z_0")
FAR = ("z_1", "z_3", "z_2")
MIX = ("z_0", "x_high", "y_high", "x_low", "y_low")
ROW_T = 128
HALF = 64
QUARTER = 32
TILE = 512

VMEM = pl.BlockSpec(memory_space=pltpu.VMEM)
SMEM = pl.BlockSpec(memory_space=pltpu.SMEM)
PARAMS = pltpu.CompilerParams(vmem_limit_bytes=16 * 1024 * 1024)


def lower_lanes(shape, width):
    return (lax.broadcasted_iota(jnp.int32, shape, 1) // width) % 2 == 0


def swapped(first, second, width):
    low = lower_lanes(first.shape, width)
    return (
        jnp.where(low, first, pltpu.roll(second, width, 1)),
        jnp.where(low, pltpu.roll(first, ROW_T - width, 1), second),
    )


def lane_blocks_transposed(tiles):
    a0, a2 = swapped(tiles[0], tiles[2], HALF)
    a1, a3 = swapped(tiles[1], tiles[3], HALF)
    return (*swapped(a0, a1, QUARTER), *swapped(a2, a3, QUARTER))


PLACES = (0, ROW_T, HALF, ROW_T + HALF)


def tile_from_pieces(ref, group):
    return lane_blocks_transposed([ref[4 * group + piece] for piece in range(4)])


def column_tile(block, half, step, reach_ref, sigma, hist_ref, out_ref, edge_ref=None):
    past_loc, tiles = hist_ref.shape[0] // ROW_T, TILE // ROW_T
    steps = hist_ref.shape[1] // 2 // TILE
    start = pl.multiple_of((half * steps + step) * TILE, TILE)
    tile_0 = (lax.axis_index(SECOND) * 2 * steps + half * steps + step) * tiles
    columns = []
    for tile in range(tiles):
        live = reach_ref[block, tile_0 + tile] - lax.axis_index(HIST) * past_loc
        parts = []
        for past in range(past_loc):
            keep = jnp.full((1, ROW_T), jnp.where(past < live, 1.0, 0.0), jnp.float32).astype(hist_ref.dtype)
            part = hist_ref[past * ROW_T : (past + 1) * ROW_T, pl.ds(start + tile * ROW_T, ROW_T)]
            parts.append(part * keep)
        columns.append(jnp.concatenate(parts, 0))
    masked = jnp.concatenate(columns, 1)
    term = jnp.dot(sigma[...], masked, preferred_element_type=jnp.float32)
    for tile in range(tiles):
        parts = [term[at : at + HALF, tile * ROW_T : (tile + 1) * ROW_T] for at in PLACES]
        if edge_ref is not None:
            adds = lax.axis_index(HIST[:4]) == 0
            for part in (0, 2):
                edge = edge_ref[PLACES[part] : PLACES[part] + HALF, pl.ds(start + tile * ROW_T, ROW_T)]
                parts[part] = parts[part] + jnp.where(adds, edge.astype(jnp.float32), 0.0)
        for piece, value in enumerate(lane_blocks_transposed([part.astype(out_ref.dtype) for part in parts])):
            out_ref[(step * tiles + tile) * 4 + piece] = value.astype(out_ref.dtype)


def memory_kernel(block, first_half, with_edge, reach_ref, sigma_ref, hist_ref, *rest):
    own = lax.axis_index("c")
    half = 1 - own if first_half else own
    edge_ref, outs = (rest[0], rest[1:]) if with_edge else (None, rest)
    sigma = sigma_ref
    if first_half:
        sigma = outs[1]
        for group in range(sigma_ref.shape[0] // 4):
            for at, value in zip(PLACES, tile_from_pieces(sigma_ref, group)):
                sigma[at : at + HALF, group * ROW_T : (group + 1) * ROW_T] = value.astype(sigma.dtype)
    for step in range(hist_ref.shape[1] // 2 // TILE):
        column_tile(block, half, step, reach_ref, sigma, hist_ref, outs[0], edge_ref)


def product_cost(rows, cols):
    return pl.CostEstimate(flops=512 * rows * cols, bytes_accessed=4 * rows * cols, transcendentals=0)


def pieces_shape(cols):
    return jax.ShapeDtypeStruct((cols // QUARTER, HALF, ROW_T), jnp.bfloat16)


def memory_terms(block, first_half, reach, sigma, history, edge=None):
    rows, cols = history.shape
    extra = () if edge is None else (edge,)
    joined = (jax.ShapeDtypeStruct((2 * ROW_T, rows), jnp.bfloat16),) if first_half else ()
    return pl.pallas_call(
        functools.partial(memory_kernel, block, first_half, edge is not None),
        out_shape=(pieces_shape(cols // 2), *joined),
        in_specs=[SMEM, VMEM, VMEM] + [VMEM] * len(extra),
        out_specs=(VMEM,) * (1 + len(joined)),
        cost_estimate=product_cost(rows, cols // 2),
        compiler_params=PARAMS,
        name=f"memory_{block}_{int(first_half)}",
    )(reach, sigma, history, *extra)


def first_kernel(reach_hbm, sigma_hbm, hist_hbm, out_ref, hist_ref, sigma_ref, reach_ref, sems):
    steps = hist_hbm.shape[1] // 2 // TILE
    own = lax.axis_index("c")
    copies = [
        pltpu.make_async_copy(reach_hbm, reach_ref, sems.at[0]),
        pltpu.make_async_copy(sigma_hbm, sigma_ref, sems.at[1]),
    ]
    for half in (1 - own, own):
        for step in range(steps):
            part = pl.ds(pl.multiple_of((half * steps + step) * TILE, TILE), TILE)
            copies.append(
                pltpu.make_async_copy(hist_hbm.at[:, part], hist_ref.at[:, part], sems.at[len(copies)])
            )
    for copy in copies:
        copy.start()
    copies[0].wait()
    copies[1].wait()
    for step in range(steps):
        copies[2 + step].wait()
        column_tile(0, 1 - own, step, reach_ref, sigma_ref, hist_ref, out_ref)
    for step in range(steps):
        copies[2 + steps + step].wait()


def first_terms(reach, sigma, history):
    rows, cols = history.shape
    there = pl.BlockSpec(memory_space=pltpu.HBM)
    return pl.pallas_call(
        first_kernel,
        out_shape=(
            pieces_shape(cols // 2),
            jax.ShapeDtypeStruct(history.shape, history.dtype),
            jax.ShapeDtypeStruct(sigma.shape, sigma.dtype),
        ),
        in_specs=[there, there, there],
        out_specs=(VMEM, VMEM, VMEM),
        scratch_shapes=[
            pltpu.SMEM(reach.shape, reach.dtype),
            pltpu.SemaphoreType.DMA((2 + cols // TILE,)),
        ],
        cost_estimate=product_cost(rows, cols // 2),
        compiler_params=PARAMS,
        name="memory_first",
    )(*(pltpu.with_memory_space_constraint(value, pltpu.HBM) for value in (reach, sigma, history)))


def in_two(value):
    high = value.astype(jnp.bfloat16)
    return high, (value - high.astype(jnp.float32)).astype(jnp.bfloat16)


def product(left, value):
    right = in_two(value)
    dot = functools.partial(jnp.dot, preferred_element_type=jnp.float32)
    return dot(left[0], right[0]) + (dot(left[0], right[1]) + dot(left[1], right[0]))


def step_kernel(first, last, terms_ref, step_ref, coupling_ref, *refs):
    count = terms_ref.shape[0] // 2
    sums = []
    for plane in range(2):
        total = terms_ref[plane * count].astype(jnp.float32)
        for place in range(1, count):
            total = total + terms_ref[plane * count + place].astype(jnp.float32)
        sums.append(total)
    source = jnp.concatenate(swapped(*sums, HALF), 0)
    step_0 = lower_lanes(source.shape, QUARTER)
    outs = refs
    if not first:
        source = source + jnp.where(step_0, pltpu.roll(refs[0][...], ROW_T - QUARTER, 1), 0.0)
        outs = refs[1:]
    operator = in_two(step_ref[...])
    moved = product(operator, source)
    rows = moved + product(operator, jnp.where(step_0, 0.0, pltpu.roll(moved, QUARTER, 1)))
    result = rows
    if not last:
        weights = jnp.broadcast_to(coupling_ref[...], rows.shape).T
        square = rows * rows
        result = weights * rows * square / (1.0 + square)
        outs[1][...] = rows
    planes = [value.astype(jnp.bfloat16) for value in swapped(result[:HALF], result[HALF:], HALF)]
    for plane in range(2):
        for copy in range(outs[0].shape[1 if last else 0]):
            if last:
                outs[0][plane, copy] = planes[plane]
            else:
                outs[0][copy, plane] = planes[plane]


def advance(first, last, terms, green, step_inv, coupling):
    copies = (2, 16) if last else (8, 2)
    shapes = [jax.ShapeDtypeStruct((*copies, HALF, ROW_T), jnp.bfloat16)]
    if not last:
        shapes.append(jax.ShapeDtypeStruct((ROW_T, ROW_T), jnp.float32))
    args = (terms, step_inv, coupling) + (() if first else (green,))
    out = pl.pallas_call(
        functools.partial(step_kernel, first, last),
        out_shape=tuple(shapes),
        in_specs=[VMEM] * len(args),
        out_specs=(VMEM,) * len(shapes),
        compiler_params=PARAMS,
        name=f"advance_{int(first)}{int(last)}",
    )(*args)
    return out[0], (None if last else out[1])


def spread_kernel(first, pieces_ref, *refs):
    out_hbm, tile_ref, sems = refs[-3:]
    core = lax.axis_index("c")
    half = core if first else 1 - core
    groups = pieces_ref.shape[0] // 4
    copies = []
    for group in range(groups):
        for at, value in zip(PLACES, tile_from_pieces(pieces_ref, group)):
            tile_ref[at : at + HALF, group * ROW_T : (group + 1) * ROW_T] = value.astype(tile_ref.dtype)
        if group % 2:
            here = tile_ref.at[:, (group - 1) * ROW_T : (group + 1) * ROW_T]
            start = pl.multiple_of((half * groups + group - 1) * ROW_T, 2 * ROW_T)
            copies.append(pltpu.make_async_copy(here, out_hbm.at[:, pl.ds(start, 2 * ROW_T)], sems.at[group // 2]))
            copies[-1].start()
    for copy in copies:
        copy.wait()


def spread_out(pieces, result=None):
    width = pieces.shape[0] * QUARTER
    first = result is None
    hbm = pl.BlockSpec(memory_space=pltpu.HBM)
    return pl.pallas_call(
        functools.partial(spread_kernel, first),
        out_shape=jax.ShapeDtypeStruct((2 * ROW_T, 2 * width), jnp.bfloat16),
        in_specs=[VMEM] if first else [VMEM, hbm],
        out_specs=hbm,
        scratch_shapes=[pltpu.VMEM((2 * ROW_T, width), jnp.bfloat16), pltpu.SemaphoreType.DMA((width // (2 * ROW_T),))],
        input_output_aliases={} if first else {1: 0},
        cost_estimate=pl.CostEstimate(flops=0, bytes_accessed=8 * ROW_T * width, transcendentals=0),
        compiler_params=PARAMS,
        name=f"spread_{int(first)}",
    )(*((pieces,) if first else (pieces, result)))


def exchange(x, axis):
    return lax.all_to_all(x, axis, 0, 0, tiled=True)


def local(history, self_rows, edge_rows, step_inv, coupling, reach):
    swap = [(0, 1), (1, 0)]
    weights = coupling[None, :]
    green, blocks = None, reach.shape[0]
    for block in range(blocks):
        last = block + 1 == blocks
        if block == 0:
            away, held, rows = first_terms(reach, self_rows, history)
        else:
            away, rows = memory_terms(block, True, reach, rows, held)
        arrived = lax.ppermute(away, "c", swap)
        (mine,) = memory_terms(block, False, reach, rows, held, edge_rows if block == 0 else None)
        pair = (mine.astype(jnp.float32) + arrived.astype(jnp.float32)).astype(jnp.bfloat16)
        terms = exchange(pair, MIX)
        pieces, green = advance(block == 0, last, terms, green, step_inv, weights)
        if last:
            own = exchange(pieces.reshape(-1, HALF, ROW_T), MIX)
            other = lax.ppermute(own, "c", swap)
            return spread_out(other, spread_out(own))
        places = exchange(pieces, FAR).reshape(2, 2, -1, HALF, ROW_T).swapaxes(0, 1).reshape(16, HALF, ROW_T)
        rows = exchange(jnp.concatenate([places, places]), MIX)


def solution(mesh):
    torus = Mesh(mesh.devices.reshape((2,) * 9), HIST + SECOND)
    placed = (P(HIST, SECOND), P(None, HIST), P(None, SECOND), P(), P(), P())
    return jax.shard_map(local, mesh=torus, in_specs=placed, out_specs=P(None, SECOND), check_vma=False)
```

```python
import functools

import jax
import jax.numpy as jnp
from jax import lax
from jax.experimental import pallas as pl
from jax.experimental.pallas import tpu as pltpu
from jax.sharding import Mesh
from jax.sharding import PartitionSpec as P

HIST = ("x_high", "x_low", "y_high", "y_low", "c")
SECOND = ("z_3", "z_2", "z_1", "z_0")
FAR = ("z_1", "z_3", "z_2")
MIX = ("z_0", "x_high", "y_high", "x_low", "y_low")
ROW_T = 128
HALF = 64
QUARTER = 32
TILE = 512
STAGGER = 1500

VMEM = pl.BlockSpec(memory_space=pltpu.VMEM)
SMEM = pl.BlockSpec(memory_space=pltpu.SMEM)
PARAMS = pltpu.CompilerParams(vmem_limit_bytes=16 * 1024 * 1024)


def lower_lanes(shape, width):
    return (lax.broadcasted_iota(jnp.int32, shape, 1) // width) % 2 == 0


def swapped(first, second, width):
    low = lower_lanes(first.shape, width)
    return (
        jnp.where(low, first, pltpu.roll(second, width, 1)),
        jnp.where(low, pltpu.roll(first, ROW_T - width, 1), second),
    )


def lane_blocks_transposed(tiles):
    a0, a2 = swapped(tiles[0], tiles[2], HALF)
    a1, a3 = swapped(tiles[1], tiles[3], HALF)
    return (*swapped(a0, a1, QUARTER), *swapped(a2, a3, QUARTER))


PLACES = (0, ROW_T, HALF, ROW_T + HALF)


def tile_from_pieces(ref, group):
    return lane_blocks_transposed([ref[4 * group + piece] for piece in range(4)])


def column_tile(block, half, step, reach_ref, sigma, hist_ref, out_ref, edge_ref=None):
    past_loc, tiles = hist_ref.shape[0] // ROW_T, TILE // ROW_T
    steps = hist_ref.shape[1] // 2 // TILE
    start = pl.multiple_of((half * steps + step) * TILE, TILE)
    tile_0 = (lax.axis_index(SECOND) * 2 * steps + half * steps + step) * tiles
    columns = []
    for tile in range(tiles):
        live = reach_ref[block, tile_0 + tile] - lax.axis_index(HIST) * past_loc
        parts = []
        for past in range(past_loc):
            keep = jnp.full((1, ROW_T), jnp.where(past < live, 1.0, 0.0), jnp.float32).astype(hist_ref.dtype)
            part = hist_ref[past * ROW_T : (past + 1) * ROW_T, pl.ds(start + tile * ROW_T, ROW_T)]
            parts.append(part * keep)
        columns.append(jnp.concatenate(parts, 0))
    masked = jnp.concatenate(columns, 1)
    term = jnp.dot(sigma[...], masked, preferred_element_type=jnp.float32)
    for tile in range(tiles):
        parts = [term[at : at + HALF, tile * ROW_T : (tile + 1) * ROW_T] for at in PLACES]
        if edge_ref is not None:
            adds = lax.axis_index(HIST[:4]) == 0
            for part in (0, 2):
                edge = edge_ref[PLACES[part] : PLACES[part] + HALF, pl.ds(start + tile * ROW_T, ROW_T)]
                parts[part] = parts[part] + jnp.where(adds, edge.astype(jnp.float32), 0.0)
        for piece, value in enumerate(lane_blocks_transposed([part.astype(out_ref.dtype) for part in parts])):
            out_ref[(step * tiles + tile) * 4 + piece] = value.astype(out_ref.dtype)


def memory_kernel(block, first_half, with_edge, reach_ref, sigma_ref, hist_ref, *rest):
    own = lax.axis_index("c")
    half = 1 - own if first_half else own
    edge_ref, outs = (rest[0], rest[1:]) if with_edge else (None, rest)
    sigma = sigma_ref
    if first_half:
        sigma = outs[1]
        for group in range(sigma_ref.shape[0] // 4):
            for at, value in zip(PLACES, tile_from_pieces(sigma_ref, group)):
                sigma[at : at + HALF, group * ROW_T : (group + 1) * ROW_T] = value.astype(sigma.dtype)
    for step in range(hist_ref.shape[1] // 2 // TILE):
        column_tile(block, half, step, reach_ref, sigma, hist_ref, outs[0], edge_ref)


def product_cost(rows, cols):
    return pl.CostEstimate(flops=512 * rows * cols, bytes_accessed=4 * rows * cols, transcendentals=0)


def pieces_shape(cols):
    return jax.ShapeDtypeStruct((cols // QUARTER, HALF, ROW_T), jnp.bfloat16)


def memory_terms(block, first_half, reach, sigma, history, edge=None):
    rows, cols = history.shape
    extra = () if edge is None else (edge,)
    joined = (jax.ShapeDtypeStruct((2 * ROW_T, rows), jnp.bfloat16),) if first_half else ()
    return pl.pallas_call(
        functools.partial(memory_kernel, block, first_half, edge is not None),
        out_shape=(pieces_shape(cols // 2), *joined),
        in_specs=[SMEM, VMEM, VMEM] + [VMEM] * len(extra),
        out_specs=(VMEM,) * (1 + len(joined)),
        cost_estimate=product_cost(rows, cols // 2),
        compiler_params=PARAMS,
        name=f"memory_{block}_{int(first_half)}",
    )(reach, sigma, history, *extra)


def first_kernel(reach_hbm, sigma_hbm, hist_hbm, out_ref, hist_ref, sigma_ref, reach_ref, sems):
    steps = hist_hbm.shape[1] // 2 // TILE
    own = lax.axis_index("c")
    copies = [
        pltpu.make_async_copy(reach_hbm, reach_ref, sems.at[0]),
        pltpu.make_async_copy(sigma_hbm, sigma_ref, sems.at[1]),
    ]
    for half in (1 - own, own):
        for step in range(steps):
            part = pl.ds(pl.multiple_of((half * steps + step) * TILE, TILE), TILE)
            copies.append(
                pltpu.make_async_copy(hist_hbm.at[:, part], hist_ref.at[:, part], sems.at[len(copies)])
            )
    for copy in copies:
        copy.start()
    copies[0].wait()
    copies[1].wait()
    for step in range(steps):
        copies[2 + step].wait()
        column_tile(0, 1 - own, step, reach_ref, sigma_ref, hist_ref, out_ref)
    for step in range(steps):
        copies[2 + steps + step].wait()


def first_terms(reach, sigma, history):
    rows, cols = history.shape
    there = pl.BlockSpec(memory_space=pltpu.HBM)
    return pl.pallas_call(
        first_kernel,
        out_shape=(
            pieces_shape(cols // 2),
            jax.ShapeDtypeStruct(history.shape, history.dtype),
            jax.ShapeDtypeStruct(sigma.shape, sigma.dtype),
        ),
        in_specs=[there, there, there],
        out_specs=(VMEM, VMEM, VMEM),
        scratch_shapes=[
            pltpu.SMEM(reach.shape, reach.dtype),
            pltpu.SemaphoreType.DMA((2 + cols // TILE,)),
        ],
        cost_estimate=product_cost(rows, cols // 2),
        compiler_params=PARAMS,
        name="memory_first",
    )(*(pltpu.with_memory_space_constraint(value, pltpu.HBM) for value in (reach, sigma, history)))


def in_two(value):
    high = value.astype(jnp.bfloat16)
    return high, (value - high.astype(jnp.float32)).astype(jnp.bfloat16)


def product(left, value):
    right = in_two(value)
    dot = functools.partial(jnp.dot, preferred_element_type=jnp.float32)
    return dot(left[0], right[0]) + (dot(left[0], right[1]) + dot(left[1], right[0]))


def step_kernel(first, last, terms_ref, step_ref, coupling_ref, *refs):
    count = terms_ref.shape[0] // 2
    sums = []
    for plane in range(2):
        total = terms_ref[plane * count].astype(jnp.float32)
        for place in range(1, count):
            total = total + terms_ref[plane * count + place].astype(jnp.float32)
        sums.append(total)
    source = jnp.concatenate(swapped(*sums, HALF), 0)
    step_0 = lower_lanes(source.shape, QUARTER)
    outs = refs
    if not first:
        source = source + jnp.where(step_0, pltpu.roll(refs[0][...], ROW_T - QUARTER, 1), 0.0)
        outs = refs[1:]
    operator = in_two(step_ref[...])
    moved = product(operator, source)
    rows = moved + product(operator, jnp.where(step_0, 0.0, pltpu.roll(moved, QUARTER, 1)))
    result = rows
    if not last:
        weights = jnp.broadcast_to(coupling_ref[...], rows.shape).T
        square = rows * rows
        result = weights * rows * square / (1.0 + square)
        outs[1][...] = rows
    if not last:

        @pl.when(lax.axis_index("c") == 1)
        def _():
            pl.delay(STAGGER)

    planes = [value.astype(jnp.bfloat16) for value in swapped(result[:HALF], result[HALF:], HALF)]
    for plane in range(2):
        for copy in range(outs[0].shape[1 if last else 0]):
            if last:
                outs[0][plane, copy] = planes[plane]
            else:
                outs[0][copy, plane] = planes[plane]


def advance(first, last, terms, green, step_inv, coupling):
    copies = (2, 16) if last else (8, 2)
    shapes = [jax.ShapeDtypeStruct((*copies, HALF, ROW_T), jnp.bfloat16)]
    if not last:
        shapes.append(jax.ShapeDtypeStruct((ROW_T, ROW_T), jnp.float32))
    args = (terms, step_inv, coupling) + (() if first else (green,))
    out = pl.pallas_call(
        functools.partial(step_kernel, first, last),
        out_shape=tuple(shapes),
        in_specs=[VMEM] * len(args),
        out_specs=(VMEM,) * len(shapes),
        compiler_params=PARAMS,
        name=f"advance_{int(first)}{int(last)}",
    )(*args)
    return out[0], (None if last else out[1])


def spread_kernel(first, pieces_ref, *refs):
    out_hbm, tile_ref, sems = refs[-3:]
    core = lax.axis_index("c")
    half = core if first else 1 - core
    groups = pieces_ref.shape[0] // 4
    copies = []
    for group in range(groups):
        for at, value in zip(PLACES, tile_from_pieces(pieces_ref, group)):
            tile_ref[at : at + HALF, group * ROW_T : (group + 1) * ROW_T] = value.astype(tile_ref.dtype)
        if group % 2:
            here = tile_ref.at[:, (group - 1) * ROW_T : (group + 1) * ROW_T]
            start = pl.multiple_of((half * groups + group - 1) * ROW_T, 2 * ROW_T)
            copies.append(pltpu.make_async_copy(here, out_hbm.at[:, pl.ds(start, 2 * ROW_T)], sems.at[group // 2]))
            copies[-1].start()
    for copy in copies:
        copy.wait()


def spread_out(pieces, result=None):
    width = pieces.shape[0] * QUARTER
    first = result is None
    hbm = pl.BlockSpec(memory_space=pltpu.HBM)
    return pl.pallas_call(
        functools.partial(spread_kernel, first),
        out_shape=jax.ShapeDtypeStruct((2 * ROW_T, 2 * width), jnp.bfloat16),
        in_specs=[VMEM] if first else [VMEM, hbm],
        out_specs=hbm,
        scratch_shapes=[pltpu.VMEM((2 * ROW_T, width), jnp.bfloat16), pltpu.SemaphoreType.DMA((width // (2 * ROW_T),))],
        input_output_aliases={} if first else {1: 0},
        cost_estimate=pl.CostEstimate(flops=0, bytes_accessed=8 * ROW_T * width, transcendentals=0),
        compiler_params=PARAMS,
        name=f"spread_{int(first)}",
    )(*((pieces,) if first else (pieces, result)))


def exchange(x, axis):
    return lax.all_to_all(x, axis, 0, 0, tiled=True)


def local(history, self_rows, edge_rows, step_inv, coupling, reach):
    swap = [(0, 1), (1, 0)]
    weights = coupling[None, :]
    green, blocks = None, reach.shape[0]
    for block in range(blocks):
        last = block + 1 == blocks
        if block == 0:
            away, held, rows = first_terms(reach, self_rows, history)
        else:
            away, rows = memory_terms(block, True, reach, rows, held)
        arrived = lax.ppermute(away, "c", swap)
        (mine,) = memory_terms(block, False, reach, rows, held, edge_rows if block == 0 else None)
        pair = (mine.astype(jnp.float32) + arrived.astype(jnp.float32)).astype(jnp.bfloat16)
        terms = exchange(pair, MIX)
        pieces, green = advance(block == 0, last, terms, green, step_inv, weights)
        if last:
            own = exchange(pieces.reshape(-1, HALF, ROW_T), MIX)
            other = lax.ppermute(own, "c", swap)
            return spread_out(other, spread_out(own))
        places = exchange(pieces, FAR).reshape(2, 2, -1, HALF, ROW_T).swapaxes(0, 1).reshape(16, HALF, ROW_T)
        rows = exchange(jnp.concatenate([places, places]), MIX)


def solution(mesh):
    torus = Mesh(mesh.devices.reshape((2,) * 9), HIST + SECOND)
    placed = (P(HIST, SECOND), P(None, HIST), P(None, SECOND), P(), P(), P())
    return jax.shard_map(local, mesh=torus, in_specs=placed, out_specs=P(None, SECOND), check_vma=False)
```

```python
import functools

import jax
import jax.numpy as jnp
from jax import lax
from jax.experimental import pallas as pl
from jax.experimental.pallas import tpu as pltpu
from jax.sharding import Mesh
from jax.sharding import PartitionSpec as P

HIST = ("x_high", "x_low", "y_high", "y_low", "c")
SECOND = ("z_3", "z_2", "z_1", "z_0")
FAR = ("z_1", "z_3", "z_2")
MIX = ("z_0", "x_high", "y_high", "x_low", "y_low")
ROW_T = 128
HALF = 64
QUARTER = 32
TILE = 512
STAGGER = 1000

VMEM = pl.BlockSpec(memory_space=pltpu.VMEM)
SMEM = pl.BlockSpec(memory_space=pltpu.SMEM)
PARAMS = pltpu.CompilerParams(vmem_limit_bytes=16 * 1024 * 1024)


def lower_lanes(shape, width):
    return (lax.broadcasted_iota(jnp.int32, shape, 1) // width) % 2 == 0


def swapped(first, second, width):
    low = lower_lanes(first.shape, width)
    return (
        jnp.where(low, first, pltpu.roll(second, width, 1)),
        jnp.where(low, pltpu.roll(first, ROW_T - width, 1), second),
    )


def lane_blocks_transposed(tiles):
    a0, a2 = swapped(tiles[0], tiles[2], HALF)
    a1, a3 = swapped(tiles[1], tiles[3], HALF)
    return (*swapped(a0, a1, QUARTER), *swapped(a2, a3, QUARTER))


PLACES = (0, ROW_T, HALF, ROW_T + HALF)


def tile_from_pieces(ref, group):
    return lane_blocks_transposed([ref[4 * group + piece] for piece in range(4)])


def column_tile(block, half, step, reach_ref, sigma, hist_ref, out_ref, edge_ref=None):
    past_loc, tiles = hist_ref.shape[0] // ROW_T, TILE // ROW_T
    steps = hist_ref.shape[1] // 2 // TILE
    start = pl.multiple_of((half * steps + step) * TILE, TILE)
    tile_0 = (lax.axis_index(SECOND) * 2 * steps + half * steps + step) * tiles
    columns = []
    for tile in range(tiles):
        live = reach_ref[block, tile_0 + tile] - lax.axis_index(HIST) * past_loc
        parts = []
        for past in range(past_loc):
            keep = jnp.full((1, ROW_T), jnp.where(past < live, 1.0, 0.0), jnp.float32).astype(hist_ref.dtype)
            part = hist_ref[past * ROW_T : (past + 1) * ROW_T, pl.ds(start + tile * ROW_T, ROW_T)]
            parts.append(part * keep)
        columns.append(jnp.concatenate(parts, 0))
    masked = jnp.concatenate(columns, 1)
    term = jnp.dot(sigma[...], masked, preferred_element_type=jnp.float32)
    for tile in range(tiles):
        parts = [term[at : at + HALF, tile * ROW_T : (tile + 1) * ROW_T] for at in PLACES]
        if edge_ref is not None:
            adds = lax.axis_index(HIST[:4]) == 0
            for part in (0, 2):
                edge = edge_ref[PLACES[part] : PLACES[part] + HALF, pl.ds(start + tile * ROW_T, ROW_T)]
                parts[part] = parts[part] + jnp.where(adds, edge.astype(jnp.float32), 0.0)
        for piece, value in enumerate(lane_blocks_transposed([part.astype(out_ref.dtype) for part in parts])):
            out_ref[(step * tiles + tile) * 4 + piece] = value.astype(out_ref.dtype)


def memory_kernel(block, first_half, with_edge, reach_ref, sigma_ref, hist_ref, *rest):
    own = lax.axis_index("c")
    half = 1 - own if first_half else own
    edge_ref, outs = (rest[0], rest[1:]) if with_edge else (None, rest)
    sigma = sigma_ref
    if first_half:
        sigma = outs[1]
        for group in range(sigma_ref.shape[0] // 4):
            for at, value in zip(PLACES, tile_from_pieces(sigma_ref, group)):
                sigma[at : at + HALF, group * ROW_T : (group + 1) * ROW_T] = value.astype(sigma.dtype)
    for step in range(hist_ref.shape[1] // 2 // TILE):
        column_tile(block, half, step, reach_ref, sigma, hist_ref, outs[0], edge_ref)
    if not first_half:

        @pl.when(own == 0)
        def _():
            pl.delay(STAGGER)


def product_cost(rows, cols):
    return pl.CostEstimate(flops=512 * rows * cols, bytes_accessed=4 * rows * cols, transcendentals=0)


def pieces_shape(cols):
    return jax.ShapeDtypeStruct((cols // QUARTER, HALF, ROW_T), jnp.bfloat16)


def memory_terms(block, first_half, reach, sigma, history, edge=None):
    rows, cols = history.shape
    extra = () if edge is None else (edge,)
    joined = (jax.ShapeDtypeStruct((2 * ROW_T, rows), jnp.bfloat16),) if first_half else ()
    return pl.pallas_call(
        functools.partial(memory_kernel, block, first_half, edge is not None),
        out_shape=(pieces_shape(cols // 2), *joined),
        in_specs=[SMEM, VMEM, VMEM] + [VMEM] * len(extra),
        out_specs=(VMEM,) * (1 + len(joined)),
        cost_estimate=product_cost(rows, cols // 2),
        compiler_params=PARAMS,
        name=f"memory_{block}_{int(first_half)}",
    )(reach, sigma, history, *extra)


def first_kernel(reach_hbm, sigma_hbm, hist_hbm, out_ref, hist_ref, sigma_ref, reach_ref, sems):
    steps = hist_hbm.shape[1] // 2 // TILE
    own = lax.axis_index("c")
    copies = [
        pltpu.make_async_copy(reach_hbm, reach_ref, sems.at[0]),
        pltpu.make_async_copy(sigma_hbm, sigma_ref, sems.at[1]),
    ]
    for half in (1 - own, own):
        for step in range(steps):
            part = pl.ds(pl.multiple_of((half * steps + step) * TILE, TILE), TILE)
            copies.append(
                pltpu.make_async_copy(hist_hbm.at[:, part], hist_ref.at[:, part], sems.at[len(copies)])
            )
    for copy in copies:
        copy.start()
    copies[0].wait()
    copies[1].wait()
    for step in range(steps):
        copies[2 + step].wait()
        column_tile(0, 1 - own, step, reach_ref, sigma_ref, hist_ref, out_ref)
    for step in range(steps):
        copies[2 + steps + step].wait()


def first_terms(reach, sigma, history):
    rows, cols = history.shape
    there = pl.BlockSpec(memory_space=pltpu.HBM)
    return pl.pallas_call(
        first_kernel,
        out_shape=(
            pieces_shape(cols // 2),
            jax.ShapeDtypeStruct(history.shape, history.dtype),
            jax.ShapeDtypeStruct(sigma.shape, sigma.dtype),
        ),
        in_specs=[there, there, there],
        out_specs=(VMEM, VMEM, VMEM),
        scratch_shapes=[
            pltpu.SMEM(reach.shape, reach.dtype),
            pltpu.SemaphoreType.DMA((2 + cols // TILE,)),
        ],
        cost_estimate=product_cost(rows, cols // 2),
        compiler_params=PARAMS,
        name="memory_first",
    )(*(pltpu.with_memory_space_constraint(value, pltpu.HBM) for value in (reach, sigma, history)))


def in_two(value):
    high = value.astype(jnp.bfloat16)
    return high, (value - high.astype(jnp.float32)).astype(jnp.bfloat16)


def product(left, value):
    right = in_two(value)
    dot = functools.partial(jnp.dot, preferred_element_type=jnp.float32)
    return dot(left[0], right[0]) + (dot(left[0], right[1]) + dot(left[1], right[0]))


def step_kernel(first, last, terms_ref, step_ref, coupling_ref, *refs):
    count = terms_ref.shape[0] // 2
    sums = []
    for plane in range(2):
        total = terms_ref[plane * count].astype(jnp.float32)
        for place in range(1, count):
            total = total + terms_ref[plane * count + place].astype(jnp.float32)
        sums.append(total)
    source = jnp.concatenate(swapped(*sums, HALF), 0)
    step_0 = lower_lanes(source.shape, QUARTER)
    outs = refs
    if not first:
        source = source + jnp.where(step_0, pltpu.roll(refs[0][...], ROW_T - QUARTER, 1), 0.0)
        outs = refs[1:]
    operator = in_two(step_ref[...])
    moved = product(operator, source)
    rows = moved + product(operator, jnp.where(step_0, 0.0, pltpu.roll(moved, QUARTER, 1)))
    result = rows
    if not last:
        weights = jnp.broadcast_to(coupling_ref[...], rows.shape).T
        square = rows * rows
        result = weights * rows * square / (1.0 + square)
        outs[1][...] = rows
    planes = [value.astype(jnp.bfloat16) for value in swapped(result[:HALF], result[HALF:], HALF)]
    for plane in range(2):
        for copy in range(outs[0].shape[1 if last else 0]):
            if last:
                outs[0][plane, copy] = planes[plane]
            else:
                outs[0][copy, plane] = planes[plane]


def advance(first, last, terms, green, step_inv, coupling):
    copies = (2, 16) if last else (8, 2)
    shapes = [jax.ShapeDtypeStruct((*copies, HALF, ROW_T), jnp.bfloat16)]
    if not last:
        shapes.append(jax.ShapeDtypeStruct((ROW_T, ROW_T), jnp.float32))
    args = (terms, step_inv, coupling) + (() if first else (green,))
    out = pl.pallas_call(
        functools.partial(step_kernel, first, last),
        out_shape=tuple(shapes),
        in_specs=[VMEM] * len(args),
        out_specs=(VMEM,) * len(shapes),
        compiler_params=PARAMS,
        name=f"advance_{int(first)}{int(last)}",
    )(*args)
    return out[0], (None if last else out[1])


def spread_kernel(first, pieces_ref, *refs):
    out_hbm, tile_ref, sems = refs[-3:]
    core = lax.axis_index("c")
    half = core if first else 1 - core
    groups = pieces_ref.shape[0] // 4
    copies = []
    for group in range(groups):
        for at, value in zip(PLACES, tile_from_pieces(pieces_ref, group)):
            tile_ref[at : at + HALF, group * ROW_T : (group + 1) * ROW_T] = value.astype(tile_ref.dtype)
        if group % 2:
            here = tile_ref.at[:, (group - 1) * ROW_T : (group + 1) * ROW_T]
            start = pl.multiple_of((half * groups + group - 1) * ROW_T, 2 * ROW_T)
            copies.append(pltpu.make_async_copy(here, out_hbm.at[:, pl.ds(start, 2 * ROW_T)], sems.at[group // 2]))
            copies[-1].start()
    for copy in copies:
        copy.wait()


def spread_out(pieces, result=None):
    width = pieces.shape[0] * QUARTER
    first = result is None
    hbm = pl.BlockSpec(memory_space=pltpu.HBM)
    return pl.pallas_call(
        functools.partial(spread_kernel, first),
        out_shape=jax.ShapeDtypeStruct((2 * ROW_T, 2 * width), jnp.bfloat16),
        in_specs=[VMEM] if first else [VMEM, hbm],
        out_specs=hbm,
        scratch_shapes=[pltpu.VMEM((2 * ROW_T, width), jnp.bfloat16), pltpu.SemaphoreType.DMA((width // (2 * ROW_T),))],
        input_output_aliases={} if first else {1: 0},
        cost_estimate=pl.CostEstimate(flops=0, bytes_accessed=8 * ROW_T * width, transcendentals=0),
        compiler_params=PARAMS,
        name=f"spread_{int(first)}",
    )(*((pieces,) if first else (pieces, result)))


def exchange(x, axis):
    return lax.all_to_all(x, axis, 0, 0, tiled=True)


def local(history, self_rows, edge_rows, step_inv, coupling, reach):
    swap = [(0, 1), (1, 0)]
    weights = coupling[None, :]
    green, blocks = None, reach.shape[0]
    for block in range(blocks):
        last = block + 1 == blocks
        if block == 0:
            away, held, rows = first_terms(reach, self_rows, history)
        else:
            away, rows = memory_terms(block, True, reach, rows, held)
        arrived = lax.ppermute(away, "c", swap)
        (mine,) = memory_terms(block, False, reach, rows, held, edge_rows if block == 0 else None)
        pair = (mine.astype(jnp.float32) + arrived.astype(jnp.float32)).astype(jnp.bfloat16)
        terms = exchange(pair, MIX)
        pieces, green = advance(block == 0, last, terms, green, step_inv, weights)
        if last:
            own = exchange(pieces.reshape(-1, HALF, ROW_T), MIX)
            other = lax.ppermute(own, "c", swap)
            return spread_out(other, spread_out(own))
        places = exchange(pieces, FAR).reshape(2, 2, -1, HALF, ROW_T).swapaxes(0, 1).reshape(16, HALF, ROW_T)
        rows = exchange(jnp.concatenate([places, places]), MIX)


def solution(mesh):
    torus = Mesh(mesh.devices.reshape((2,) * 9), HIST + SECOND)
    placed = (P(HIST, SECOND), P(None, HIST), P(None, SECOND), P(), P(), P())
    return jax.shard_map(local, mesh=torus, in_specs=placed, out_specs=P(None, SECOND), check_vma=False)
```

```python
import functools

import jax
import jax.numpy as jnp
from jax import lax
from jax.experimental import pallas as pl
from jax.experimental.pallas import tpu as pltpu
from jax.sharding import Mesh
from jax.sharding import PartitionSpec as P

HIST = ("x_high", "x_low", "y_high", "y_low", "c")
SECOND = ("z_3", "z_2", "z_1", "z_0")
FAR = ("z_1", "z_3", "z_2")
MIX = ("z_0", "x_high", "y_high", "x_low", "y_low")
ROW_T = 128
HALF = 64
QUARTER = 32
TILE = 512
STAGGER = 1500

VMEM = pl.BlockSpec(memory_space=pltpu.VMEM)
SMEM = pl.BlockSpec(memory_space=pltpu.SMEM)
PARAMS = pltpu.CompilerParams(vmem_limit_bytes=16 * 1024 * 1024)


def lower_lanes(shape, width):
    return (lax.broadcasted_iota(jnp.int32, shape, 1) // width) % 2 == 0


def swapped(first, second, width):
    low = lower_lanes(first.shape, width)
    return (
        jnp.where(low, first, pltpu.roll(second, width, 1)),
        jnp.where(low, pltpu.roll(first, ROW_T - width, 1), second),
    )


def lane_blocks_transposed(tiles):
    a0, a2 = swapped(tiles[0], tiles[2], HALF)
    a1, a3 = swapped(tiles[1], tiles[3], HALF)
    return (*swapped(a0, a1, QUARTER), *swapped(a2, a3, QUARTER))


PLACES = (0, ROW_T, HALF, ROW_T + HALF)


def tile_from_pieces(ref, group):
    return lane_blocks_transposed([ref[4 * group + piece] for piece in range(4)])


def column_tile(block, half, step, reach_ref, sigma, hist_ref, out_ref, edge_ref=None):
    past_loc, tiles = hist_ref.shape[0] // ROW_T, TILE // ROW_T
    steps = hist_ref.shape[1] // 2 // TILE
    start = pl.multiple_of((half * steps + step) * TILE, TILE)
    tile_0 = (lax.axis_index(SECOND) * 2 * steps + half * steps + step) * tiles
    columns = []
    for tile in range(tiles):
        live = reach_ref[block, tile_0 + tile] - lax.axis_index(HIST) * past_loc
        parts = []
        for past in range(past_loc):
            keep = jnp.full((1, ROW_T), jnp.where(past < live, 1.0, 0.0), jnp.float32).astype(hist_ref.dtype)
            part = hist_ref[past * ROW_T : (past + 1) * ROW_T, pl.ds(start + tile * ROW_T, ROW_T)]
            parts.append(part * keep)
        columns.append(jnp.concatenate(parts, 0))
    masked = jnp.concatenate(columns, 1)
    term = jnp.dot(sigma[...], masked, preferred_element_type=jnp.float32)
    for tile in range(tiles):
        parts = [term[at : at + HALF, tile * ROW_T : (tile + 1) * ROW_T] for at in PLACES]
        if edge_ref is not None:
            adds = lax.axis_index(HIST[:4]) == 0
            for part in (0, 2):
                edge = edge_ref[PLACES[part] : PLACES[part] + HALF, pl.ds(start + tile * ROW_T, ROW_T)]
                parts[part] = parts[part] + jnp.where(adds, edge.astype(jnp.float32), 0.0)
        for piece, value in enumerate(lane_blocks_transposed([part.astype(out_ref.dtype) for part in parts])):
            out_ref[(step * tiles + tile) * 4 + piece] = value.astype(out_ref.dtype)


def memory_kernel(block, first_half, with_edge, reach_ref, sigma_ref, hist_ref, *rest):
    own = lax.axis_index("c")
    half = 1 - own if first_half else own
    edge_ref, outs = (rest[0], rest[1:]) if with_edge else (None, rest)
    sigma = sigma_ref
    if first_half:
        sigma = outs[1]
        for group in range(sigma_ref.shape[0] // 4):
            for at, value in zip(PLACES, tile_from_pieces(sigma_ref, group)):
                sigma[at : at + HALF, group * ROW_T : (group + 1) * ROW_T] = value.astype(sigma.dtype)
    for step in range(hist_ref.shape[1] // 2 // TILE):
        column_tile(block, half, step, reach_ref, sigma, hist_ref, outs[0], edge_ref)
    if not first_half:

        @pl.when(own == 0)
        def _():
            pl.delay(STAGGER)


def product_cost(rows, cols):
    return pl.CostEstimate(flops=512 * rows * cols, bytes_accessed=4 * rows * cols, transcendentals=0)


def pieces_shape(cols):
    return jax.ShapeDtypeStruct((cols // QUARTER, HALF, ROW_T), jnp.bfloat16)


def memory_terms(block, first_half, reach, sigma, history, edge=None):
    rows, cols = history.shape
    extra = () if edge is None else (edge,)
    joined = (jax.ShapeDtypeStruct((2 * ROW_T, rows), jnp.bfloat16),) if first_half else ()
    return pl.pallas_call(
        functools.partial(memory_kernel, block, first_half, edge is not None),
        out_shape=(pieces_shape(cols // 2), *joined),
        in_specs=[SMEM, VMEM, VMEM] + [VMEM] * len(extra),
        out_specs=(VMEM,) * (1 + len(joined)),
        cost_estimate=product_cost(rows, cols // 2),
        compiler_params=PARAMS,
        name=f"memory_{block}_{int(first_half)}",
    )(reach, sigma, history, *extra)


def first_kernel(reach_hbm, sigma_hbm, hist_hbm, out_ref, hist_ref, sigma_ref, reach_ref, sems):
    steps = hist_hbm.shape[1] // 2 // TILE
    own = lax.axis_index("c")
    copies = [
        pltpu.make_async_copy(reach_hbm, reach_ref, sems.at[0]),
        pltpu.make_async_copy(sigma_hbm, sigma_ref, sems.at[1]),
    ]
    for half in (1 - own, own):
        for step in range(steps):
            part = pl.ds(pl.multiple_of((half * steps + step) * TILE, TILE), TILE)
            copies.append(
                pltpu.make_async_copy(hist_hbm.at[:, part], hist_ref.at[:, part], sems.at[len(copies)])
            )
    for copy in copies:
        copy.start()
    copies[0].wait()
    copies[1].wait()
    for step in range(steps):
        copies[2 + step].wait()
        column_tile(0, 1 - own, step, reach_ref, sigma_ref, hist_ref, out_ref)
    for step in range(steps):
        copies[2 + steps + step].wait()


def first_terms(reach, sigma, history):
    rows, cols = history.shape
    there = pl.BlockSpec(memory_space=pltpu.HBM)
    return pl.pallas_call(
        first_kernel,
        out_shape=(
            pieces_shape(cols // 2),
            jax.ShapeDtypeStruct(history.shape, history.dtype),
            jax.ShapeDtypeStruct(sigma.shape, sigma.dtype),
        ),
        in_specs=[there, there, there],
        out_specs=(VMEM, VMEM, VMEM),
        scratch_shapes=[
            pltpu.SMEM(reach.shape, reach.dtype),
            pltpu.SemaphoreType.DMA((2 + cols // TILE,)),
        ],
        cost_estimate=product_cost(rows, cols // 2),
        compiler_params=PARAMS,
        name="memory_first",
    )(*(pltpu.with_memory_space_constraint(value, pltpu.HBM) for value in (reach, sigma, history)))


def in_two(value):
    high = value.astype(jnp.bfloat16)
    return high, (value - high.astype(jnp.float32)).astype(jnp.bfloat16)


def product(left, value):
    right = in_two(value)
    dot = functools.partial(jnp.dot, preferred_element_type=jnp.float32)
    return dot(left[0], right[0]) + (dot(left[0], right[1]) + dot(left[1], right[0]))


def step_kernel(first, last, terms_ref, step_ref, coupling_ref, *refs):
    count = terms_ref.shape[0] // 2
    sums = []
    for plane in range(2):
        total = terms_ref[plane * count].astype(jnp.float32)
        for place in range(1, count):
            total = total + terms_ref[plane * count + place].astype(jnp.float32)
        sums.append(total)
    source = jnp.concatenate(swapped(*sums, HALF), 0)
    step_0 = lower_lanes(source.shape, QUARTER)
    outs = refs
    if not first:
        source = source + jnp.where(step_0, pltpu.roll(refs[0][...], ROW_T - QUARTER, 1), 0.0)
        outs = refs[1:]
    operator = in_two(step_ref[...])
    moved = product(operator, source)
    rows = moved + product(operator, jnp.where(step_0, 0.0, pltpu.roll(moved, QUARTER, 1)))
    result = rows
    if not last:
        weights = jnp.broadcast_to(coupling_ref[...], rows.shape).T
        square = rows * rows
        result = weights * rows * square / (1.0 + square)
        outs[1][...] = rows
    planes = [value.astype(jnp.bfloat16) for value in swapped(result[:HALF], result[HALF:], HALF)]
    for plane in range(2):
        for copy in range(outs[0].shape[1 if last else 0]):
            if last:
                outs[0][plane, copy] = planes[plane]
            else:
                outs[0][copy, plane] = planes[plane]


def advance(first, last, terms, green, step_inv, coupling):
    copies = (2, 16) if last else (8, 2)
    shapes = [jax.ShapeDtypeStruct((*copies, HALF, ROW_T), jnp.bfloat16)]
    if not last:
        shapes.append(jax.ShapeDtypeStruct((ROW_T, ROW_T), jnp.float32))
    args = (terms, step_inv, coupling) + (() if first else (green,))
    out = pl.pallas_call(
        functools.partial(step_kernel, first, last),
        out_shape=tuple(shapes),
        in_specs=[VMEM] * len(args),
        out_specs=(VMEM,) * len(shapes),
        compiler_params=PARAMS,
        name=f"advance_{int(first)}{int(last)}",
    )(*args)
    return out[0], (None if last else out[1])


def spread_kernel(first, pieces_ref, *refs):
    out_hbm, tile_ref, sems = refs[-3:]
    core = lax.axis_index("c")
    half = core if first else 1 - core
    groups = pieces_ref.shape[0] // 4
    copies = []
    for group in range(groups):
        for at, value in zip(PLACES, tile_from_pieces(pieces_ref, group)):
            tile_ref[at : at + HALF, group * ROW_T : (group + 1) * ROW_T] = value.astype(tile_ref.dtype)
        if group % 2:
            here = tile_ref.at[:, (group - 1) * ROW_T : (group + 1) * ROW_T]
            start = pl.multiple_of((half * groups + group - 1) * ROW_T, 2 * ROW_T)
            copies.append(pltpu.make_async_copy(here, out_hbm.at[:, pl.ds(start, 2 * ROW_T)], sems.at[group // 2]))
            copies[-1].start()
    for copy in copies:
        copy.wait()


def spread_out(pieces, result=None):
    width = pieces.shape[0] * QUARTER
    first = result is None
    hbm = pl.BlockSpec(memory_space=pltpu.HBM)
    return pl.pallas_call(
        functools.partial(spread_kernel, first),
        out_shape=jax.ShapeDtypeStruct((2 * ROW_T, 2 * width), jnp.bfloat16),
        in_specs=[VMEM] if first else [VMEM, hbm],
        out_specs=hbm,
        scratch_shapes=[pltpu.VMEM((2 * ROW_T, width), jnp.bfloat16), pltpu.SemaphoreType.DMA((width // (2 * ROW_T),))],
        input_output_aliases={} if first else {1: 0},
        cost_estimate=pl.CostEstimate(flops=0, bytes_accessed=8 * ROW_T * width, transcendentals=0),
        compiler_params=PARAMS,
        name=f"spread_{int(first)}",
    )(*((pieces,) if first else (pieces, result)))


def exchange(x, axis):
    return lax.all_to_all(x, axis, 0, 0, tiled=True)


def local(history, self_rows, edge_rows, step_inv, coupling, reach):
    swap = [(0, 1), (1, 0)]
    weights = coupling[None, :]
    green, blocks = None, reach.shape[0]
    for block in range(blocks):
        last = block + 1 == blocks
        if block == 0:
            away, held, rows = first_terms(reach, self_rows, history)
        else:
            away, rows = memory_terms(block, True, reach, rows, held)
        arrived = lax.ppermute(away, "c", swap)
        (mine,) = memory_terms(block, False, reach, rows, held, edge_rows if block == 0 else None)
        pair = (mine.astype(jnp.float32) + arrived.astype(jnp.float32)).astype(jnp.bfloat16)
        terms = exchange(pair, MIX)
        pieces, green = advance(block == 0, last, terms, green, step_inv, weights)
        if last:
            own = exchange(pieces.reshape(-1, HALF, ROW_T), MIX)
            other = lax.ppermute(own, "c", swap)
            return spread_out(other, spread_out(own))
        places = exchange(pieces, FAR).reshape(2, 2, -1, HALF, ROW_T).swapaxes(0, 1).reshape(16, HALF, ROW_T)
        rows = exchange(jnp.concatenate([places, places]), MIX)


def solution(mesh):
    torus = Mesh(mesh.devices.reshape((2,) * 9), HIST + SECOND)
    placed = (P(HIST, SECOND), P(None, HIST), P(None, SECOND), P(), P(), P())
    return jax.shard_map(local, mesh=torus, in_specs=placed, out_specs=P(None, SECOND), check_vma=False)
```

```python
import functools

import jax
import jax.numpy as jnp
from jax import lax
from jax.experimental import pallas as pl
from jax.experimental.pallas import tpu as pltpu
from jax.sharding import Mesh
from jax.sharding import PartitionSpec as P

HIST = ("x_high", "x_low", "y_high", "y_low", "c")
SECOND = ("z_3", "z_2", "z_1", "z_0")
FAR = ("z_1", "z_3", "z_2")
MIX = ("z_0", "x_high", "y_high", "x_low", "y_low")
ROW_T = 128
HALF = 64
QUARTER = 32
TILE = 512
STAGGER = 2200

VMEM = pl.BlockSpec(memory_space=pltpu.VMEM)
SMEM = pl.BlockSpec(memory_space=pltpu.SMEM)
PARAMS = pltpu.CompilerParams(vmem_limit_bytes=16 * 1024 * 1024)


def lower_lanes(shape, width):
    return (lax.broadcasted_iota(jnp.int32, shape, 1) // width) % 2 == 0


def swapped(first, second, width):
    low = lower_lanes(first.shape, width)
    return (
        jnp.where(low, first, pltpu.roll(second, width, 1)),
        jnp.where(low, pltpu.roll(first, ROW_T - width, 1), second),
    )


def lane_blocks_transposed(tiles):
    a0, a2 = swapped(tiles[0], tiles[2], HALF)
    a1, a3 = swapped(tiles[1], tiles[3], HALF)
    return (*swapped(a0, a1, QUARTER), *swapped(a2, a3, QUARTER))


PLACES = (0, ROW_T, HALF, ROW_T + HALF)


def tile_from_pieces(ref, group):
    return lane_blocks_transposed([ref[4 * group + piece] for piece in range(4)])


def column_tile(block, half, step, reach_ref, sigma, hist_ref, out_ref, edge_ref=None):
    past_loc, tiles = hist_ref.shape[0] // ROW_T, TILE // ROW_T
    steps = hist_ref.shape[1] // 2 // TILE
    start = pl.multiple_of((half * steps + step) * TILE, TILE)
    tile_0 = (lax.axis_index(SECOND) * 2 * steps + half * steps + step) * tiles
    columns = []
    for tile in range(tiles):
        live = reach_ref[block, tile_0 + tile] - lax.axis_index(HIST) * past_loc
        parts = []
        for past in range(past_loc):
            keep = jnp.full((1, ROW_T), jnp.where(past < live, 1.0, 0.0), jnp.float32).astype(hist_ref.dtype)
            part = hist_ref[past * ROW_T : (past + 1) * ROW_T, pl.ds(start + tile * ROW_T, ROW_T)]
            parts.append(part * keep)
        columns.append(jnp.concatenate(parts, 0))
    masked = jnp.concatenate(columns, 1)
    term = jnp.dot(sigma[...], masked, preferred_element_type=jnp.float32)
    for tile in range(tiles):
        parts = [term[at : at + HALF, tile * ROW_T : (tile + 1) * ROW_T] for at in PLACES]
        if edge_ref is not None:
            adds = lax.axis_index(HIST[:4]) == 0
            for part in (0, 2):
                edge = edge_ref[PLACES[part] : PLACES[part] + HALF, pl.ds(start + tile * ROW_T, ROW_T)]
                parts[part] = parts[part] + jnp.where(adds, edge.astype(jnp.float32), 0.0)
        for piece, value in enumerate(lane_blocks_transposed([part.astype(out_ref.dtype) for part in parts])):
            out_ref[(step * tiles + tile) * 4 + piece] = value.astype(out_ref.dtype)


def memory_kernel(block, first_half, with_edge, reach_ref, sigma_ref, hist_ref, *rest):
    own = lax.axis_index("c")
    half = 1 - own if first_half else own
    edge_ref, outs = (rest[0], rest[1:]) if with_edge else (None, rest)
    sigma = sigma_ref
    if first_half:
        sigma = outs[1]
        for group in range(sigma_ref.shape[0] // 4):
            for at, value in zip(PLACES, tile_from_pieces(sigma_ref, group)):
                sigma[at : at + HALF, group * ROW_T : (group + 1) * ROW_T] = value.astype(sigma.dtype)
    for step in range(hist_ref.shape[1] // 2 // TILE):
        column_tile(block, half, step, reach_ref, sigma, hist_ref, outs[0], edge_ref)
    if not first_half:

        @pl.when(own == 0)
        def _():
            pl.delay(STAGGER)


def product_cost(rows, cols):
    return pl.CostEstimate(flops=512 * rows * cols, bytes_accessed=4 * rows * cols, transcendentals=0)


def pieces_shape(cols):
    return jax.ShapeDtypeStruct((cols // QUARTER, HALF, ROW_T), jnp.bfloat16)


def memory_terms(block, first_half, reach, sigma, history, edge=None):
    rows, cols = history.shape
    extra = () if edge is None else (edge,)
    joined = (jax.ShapeDtypeStruct((2 * ROW_T, rows), jnp.bfloat16),) if first_half else ()
    return pl.pallas_call(
        functools.partial(memory_kernel, block, first_half, edge is not None),
        out_shape=(pieces_shape(cols // 2), *joined),
        in_specs=[SMEM, VMEM, VMEM] + [VMEM] * len(extra),
        out_specs=(VMEM,) * (1 + len(joined)),
        cost_estimate=product_cost(rows, cols // 2),
        compiler_params=PARAMS,
        name=f"memory_{block}_{int(first_half)}",
    )(reach, sigma, history, *extra)


def first_kernel(reach_hbm, sigma_hbm, hist_hbm, out_ref, hist_ref, sigma_ref, reach_ref, sems):
    steps = hist_hbm.shape[1] // 2 // TILE
    own = lax.axis_index("c")
    copies = [
        pltpu.make_async_copy(reach_hbm, reach_ref, sems.at[0]),
        pltpu.make_async_copy(sigma_hbm, sigma_ref, sems.at[1]),
    ]
    for half in (1 - own, own):
        for step in range(steps):
            part = pl.ds(pl.multiple_of((half * steps + step) * TILE, TILE), TILE)
            copies.append(
                pltpu.make_async_copy(hist_hbm.at[:, part], hist_ref.at[:, part], sems.at[len(copies)])
            )
    for copy in copies:
        copy.start()
    copies[0].wait()
    copies[1].wait()
    for step in range(steps):
        copies[2 + step].wait()
        column_tile(0, 1 - own, step, reach_ref, sigma_ref, hist_ref, out_ref)
    for step in range(steps):
        copies[2 + steps + step].wait()


def first_terms(reach, sigma, history):
    rows, cols = history.shape
    there = pl.BlockSpec(memory_space=pltpu.HBM)
    return pl.pallas_call(
        first_kernel,
        out_shape=(
            pieces_shape(cols // 2),
            jax.ShapeDtypeStruct(history.shape, history.dtype),
            jax.ShapeDtypeStruct(sigma.shape, sigma.dtype),
        ),
        in_specs=[there, there, there],
        out_specs=(VMEM, VMEM, VMEM),
        scratch_shapes=[
            pltpu.SMEM(reach.shape, reach.dtype),
            pltpu.SemaphoreType.DMA((2 + cols // TILE,)),
        ],
        cost_estimate=product_cost(rows, cols // 2),
        compiler_params=PARAMS,
        name="memory_first",
    )(*(pltpu.with_memory_space_constraint(value, pltpu.HBM) for value in (reach, sigma, history)))


def in_two(value):
    high = value.astype(jnp.bfloat16)
    return high, (value - high.astype(jnp.float32)).astype(jnp.bfloat16)


def product(left, value):
    right = in_two(value)
    dot = functools.partial(jnp.dot, preferred_element_type=jnp.float32)
    return dot(left[0], right[0]) + (dot(left[0], right[1]) + dot(left[1], right[0]))


def step_kernel(first, last, terms_ref, step_ref, coupling_ref, *refs):
    count = terms_ref.shape[0] // 2
    sums = []
    for plane in range(2):
        total = terms_ref[plane * count].astype(jnp.float32)
        for place in range(1, count):
            total = total + terms_ref[plane * count + place].astype(jnp.float32)
        sums.append(total)
    source = jnp.concatenate(swapped(*sums, HALF), 0)
    step_0 = lower_lanes(source.shape, QUARTER)
    outs = refs
    if not first:
        source = source + jnp.where(step_0, pltpu.roll(refs[0][...], ROW_T - QUARTER, 1), 0.0)
        outs = refs[1:]
    operator = in_two(step_ref[...])
    moved = product(operator, source)
    rows = moved + product(operator, jnp.where(step_0, 0.0, pltpu.roll(moved, QUARTER, 1)))
    result = rows
    if not last:
        weights = jnp.broadcast_to(coupling_ref[...], rows.shape).T
        square = rows * rows
        result = weights * rows * square / (1.0 + square)
        outs[1][...] = rows
    planes = [value.astype(jnp.bfloat16) for value in swapped(result[:HALF], result[HALF:], HALF)]
    for plane in range(2):
        for copy in range(outs[0].shape[1 if last else 0]):
            if last:
                outs[0][plane, copy] = planes[plane]
            else:
                outs[0][copy, plane] = planes[plane]


def advance(first, last, terms, green, step_inv, coupling):
    copies = (2, 16) if last else (8, 2)
    shapes = [jax.ShapeDtypeStruct((*copies, HALF, ROW_T), jnp.bfloat16)]
    if not last:
        shapes.append(jax.ShapeDtypeStruct((ROW_T, ROW_T), jnp.float32))
    args = (terms, step_inv, coupling) + (() if first else (green,))
    out = pl.pallas_call(
        functools.partial(step_kernel, first, last),
        out_shape=tuple(shapes),
        in_specs=[VMEM] * len(args),
        out_specs=(VMEM,) * len(shapes),
        compiler_params=PARAMS,
        name=f"advance_{int(first)}{int(last)}",
    )(*args)
    return out[0], (None if last else out[1])


def spread_kernel(first, pieces_ref, *refs):
    out_hbm, tile_ref, sems = refs[-3:]
    core = lax.axis_index("c")
    half = core if first else 1 - core
    groups = pieces_ref.shape[0] // 4
    copies = []
    for group in range(groups):
        for at, value in zip(PLACES, tile_from_pieces(pieces_ref, group)):
            tile_ref[at : at + HALF, group * ROW_T : (group + 1) * ROW_T] = value.astype(tile_ref.dtype)
        if group % 2:
            here = tile_ref.at[:, (group - 1) * ROW_T : (group + 1) * ROW_T]
            start = pl.multiple_of((half * groups + group - 1) * ROW_T, 2 * ROW_T)
            copies.append(pltpu.make_async_copy(here, out_hbm.at[:, pl.ds(start, 2 * ROW_T)], sems.at[group // 2]))
            copies[-1].start()
    for copy in copies:
        copy.wait()


def spread_out(pieces, result=None):
    width = pieces.shape[0] * QUARTER
    first = result is None
    hbm = pl.BlockSpec(memory_space=pltpu.HBM)
    return pl.pallas_call(
        functools.partial(spread_kernel, first),
        out_shape=jax.ShapeDtypeStruct((2 * ROW_T, 2 * width), jnp.bfloat16),
        in_specs=[VMEM] if first else [VMEM, hbm],
        out_specs=hbm,
        scratch_shapes=[pltpu.VMEM((2 * ROW_T, width), jnp.bfloat16), pltpu.SemaphoreType.DMA((width // (2 * ROW_T),))],
        input_output_aliases={} if first else {1: 0},
        cost_estimate=pl.CostEstimate(flops=0, bytes_accessed=8 * ROW_T * width, transcendentals=0),
        compiler_params=PARAMS,
        name=f"spread_{int(first)}",
    )(*((pieces,) if first else (pieces, result)))


def exchange(x, axis):
    return lax.all_to_all(x, axis, 0, 0, tiled=True)


def local(history, self_rows, edge_rows, step_inv, coupling, reach):
    swap = [(0, 1), (1, 0)]
    weights = coupling[None, :]
    green, blocks = None, reach.shape[0]
    for block in range(blocks):
        last = block + 1 == blocks
        if block == 0:
            away, held, rows = first_terms(reach, self_rows, history)
        else:
            away, rows = memory_terms(block, True, reach, rows, held)
        arrived = lax.ppermute(away, "c", swap)
        (mine,) = memory_terms(block, False, reach, rows, held, edge_rows if block == 0 else None)
        pair = (mine.astype(jnp.float32) + arrived.astype(jnp.float32)).astype(jnp.bfloat16)
        terms = exchange(pair, MIX)
        pieces, green = advance(block == 0, last, terms, green, step_inv, weights)
        if last:
            own = exchange(pieces.reshape(-1, HALF, ROW_T), MIX)
            other = lax.ppermute(own, "c", swap)
            return spread_out(other, spread_out(own))
        places = exchange(pieces, FAR).reshape(2, 2, -1, HALF, ROW_T).swapaxes(0, 1).reshape(16, HALF, ROW_T)
        rows = exchange(jnp.concatenate([places, places]), MIX)


def solution(mesh):
    torus = Mesh(mesh.devices.reshape((2,) * 9), HIST + SECOND)
    placed = (P(HIST, SECOND), P(None, HIST), P(None, SECOND), P(), P(), P())
    return jax.shard_map(local, mesh=torus, in_specs=placed, out_specs=P(None, SECOND), check_vma=False)
```
